32 devices in a mesh: blk: 8 (over z, x), grp: 4 (over y, core).
Axes of the slice: x: 2, y: 2, z: 4, core: 2. Of those that a mesh axis runs over, the one named last changes fastest.
Arguments:
- snapshots: bfloat16 [65536, 1024], P(('grp', 'blk')), may hold values from -1200 to 1200
- start: float32 [1024, 256], replicated, may hold values from -6 to 6
- pivot_dev: int32 [32], replicated, may hold values from 0 to 31, as said below
- pivot_row: int32 [32], replicated, may hold values from 0 to 2047, as said below
Outputs:
- modes: bfloat16 [65536, 256], P(('grp', 'blk'))
- scores: float32 [65536], P(('grp', 'blk'))
- panel_basis: float32 [256, 32], replicated
The draws below stay inside these ranges and needn't reach their ends.
Inputs may be any that keep to these rules, and one draw needn't show every extreme that they name: Together with pivot_row, names 32 distinct global rows pivot_dev * 2048 + pivot_row; the first and the last global row are always among them. `pivot_row`: see pivot_dev.
All inputs are finite; a program needn't handle non-finite values.
Results may differ from the reference program's by a relative error of at most 0.0051.
Values sent between devices are 32-bit elements; how exact they have to be, the bound alone decides.
No kernel may reach another device: no remote copies, remote signals or barrier semaphores. Data moves between devices by JAX's collectives and lax.ppermute only.
A program may use at most 64 MiB of HBM per device.

```python
import math
import jax
import jax.numpy as jnp
from jax import lax

ROWS_DEV = 2048
SNAP = 1024
RANK = 256
PANEL = 32
ITERS = 4
ROWS = 65536


def draw_snapshots(key, part):
    keys = jax.random.split(jax.random.fold_in(key, 11), 3)
    positions = jnp.arange(ROWS, dtype=jnp.float32)[:, None]
    row_scale = jnp.exp(jax.random.uniform(keys[0], (ROWS, 1), jnp.float32) * math.log(10.0))
    row_scale = row_scale * jnp.exp(math.log(3.0) * positions / ROWS)
    col_scale = jnp.exp(jax.random.uniform(keys[1], (1, SNAP), jnp.float32) * math.log(10.0))
    values = jnp.clip(jax.random.normal(keys[2], (ROWS, SNAP), jnp.float32), -4.0, 4.0)
    return (values * row_scale * col_scale).astype(jnp.bfloat16)


def pivot_pairs(key):
    keys = jax.random.split(jax.random.fold_in(key, 7), 2)
    middle = jax.random.permutation(keys[0], ROWS - 2)[:PANEL - 2].astype(jnp.int32) + 1
    chosen = jnp.concatenate([jnp.array([0, ROWS - 1], jnp.int32), middle])
    chosen = chosen[jax.random.permutation(keys[1], PANEL)]
    return (chosen // ROWS_DEV, chosen % ROWS_DEV)


def draw_pivot_dev(key, part):
    return pivot_pairs(key)[0].astype(jnp.int32)


def draw_pivot_row(key, part):
    return pivot_pairs(key)[1].astype(jnp.int32)


def gaussian(rng, extent, deviation, reach, kind=jnp.bfloat16):
    result = deviation * jax.random.normal(rng, extent, jnp.float32)
    return jnp.clip(result, min=-reach, max=reach).astype(kind)


def setup_inputs(seed: int = 0) -> dict:
    splits = jax.random.split(jax.random.key(seed), 5)
    return {
        "snapshots": draw_snapshots(jax.random.fold_in(splits[4], 71), 0),
        "start": gaussian(splits[1], (SNAP, RANK), 1.0, 6.0, jnp.float32),
        "pivot_dev": draw_pivot_dev(jax.random.fold_in(splits[4], 71), 0),
        "pivot_row": draw_pivot_row(jax.random.fold_in(splits[4], 71), 0),
    }


def right_solve(factor, matrix):
    return lax.linalg.triangular_solve(factor, matrix, left_side=False, lower=True, transpose_a=True)

def reference(snapshots, start, pivot_dev, pivot_row):
    blocks = snapshots.reshape(ROWS // ROWS_DEV, ROWS_DEV, SNAP)

    def add_block(total, block_rows):
        term = lax.dot_general(block_rows.astype(jnp.float32), block_rows.astype(jnp.float32), (((0,), (0,)), ((), ())), preferred_element_type=jnp.float32)
        return (total + term, None)
    gram_full, unused = lax.scan(add_block, jnp.zeros((SNAP, SNAP), jnp.float32), blocks)
    iterate = start
    for repeat in range(ITERS):
        image = jnp.dot(gram_full, iterate, precision=lax.Precision.HIGHEST)
        square = jnp.dot(image.T, image, precision=lax.Precision.HIGHEST)
        iterate = right_solve(jnp.linalg.cholesky(square), image)
    image = jnp.dot(gram_full, iterate, precision=lax.Precision.HIGHEST)
    small_gram = jnp.dot(iterate.T, image, precision=lax.Precision.HIGHEST) / ROWS
    coef = right_solve(jnp.linalg.cholesky(small_gram), iterate).astype(jnp.bfloat16)
    basis = jnp.dot(snapshots.astype(jnp.float32), coef.astype(jnp.float32), preferred_element_type=jnp.float32)
    global_rows = (pivot_dev * ROWS_DEV + pivot_row).astype(jnp.int32)
    panel = basis[global_rows]
    panel_gram = jnp.dot(panel, panel.T, precision=lax.Precision.HIGHEST)
    panel_basis = right_solve(jnp.linalg.cholesky(panel_gram), panel.T)
    coeffs = jnp.dot(basis, panel_basis, precision=lax.Precision.HIGHEST)
    remaining = basis - jnp.dot(coeffs, panel_basis.T, precision=lax.Precision.HIGHEST)
    scores = jnp.sum(remaining * remaining, axis=1) / RANK
    return (basis.astype(jnp.bfloat16), scores, panel_basis)
```

```python
import functools
import jax
import jax.numpy as jnp
from jax import lax
from jax.experimental import pallas as pl
from jax.experimental.pallas import tpu as pltpu
from jax.sharding import PartitionSpec as P

ITERS = 4
TILE = 128
BAND = 2
BLOCK = 64
F32, BF16 = jnp.float32, jnp.bfloat16
HIGHEST = lax.Precision.HIGHEST
VMEM = pl.BlockSpec(memory_space=pltpu.VMEM)
SMEM = pl.BlockSpec(memory_space=pltpu.SMEM)


def dot(a, b, ca, cb, precision=None):
    return lax.dot_general(
        a, b, (((ca,), (cb,)), ((), ())), precision=precision, preferred_element_type=F32
    )


def split(value):
    high = value.astype(BF16)
    return high, (value - high.astype(F32)).astype(BF16)


def iota(shape, dim):
    return lax.broadcasted_iota(jnp.int32, shape, dim)


def bands_of(tiles):
    count = tiles // BAND
    outer = [0, count - 1] if count > 1 else [0]
    return outer, [band for band in range(count) if band not in outer]


def places(tiles):
    result = []
    for bands in bands_of(tiles):
        row, entries = 0, []
        for band in bands:
            for i in range(band * BAND, band * BAND + BAND):
                for j in range(i, tiles):
                    entries.append((i, j, row))
                    row += TILE
        result.append((entries, row))
    return result


def exchange_plan(mesh_shape, rows):
    grp = [("grp", 1 << b) for b in range(mesh_shape["grp"].bit_length() - 1)]
    blk = [("blk", 1 << b) for b in range(mesh_shape["blk"].bit_length() - 1)]
    rest = blk[1:] + grp[2:]
    orders = (grp[:1] + blk[:1] + grp[1:2] + rest, grp[:1] + grp[1:2] + blk[:1] + rest)
    halvings = 0
    while halvings < len(orders[0]) and all(r % (8 << (halvings + 1)) == 0 for r in rows):
        halvings += 1
    return orders, halvings


def key_of(order, halvings):
    key = jnp.int32(0)
    for axis, mask in order[:halvings]:
        key = key * 2 + jnp.where((lax.axis_index(axis) & mask) != 0, 1, 0)
    return key


def send(value, axis, mask):
    size = lax.axis_size(axis)
    return lax.ppermute(value, axis, [(i, i ^ mask) for i in range(size)])


def exchange(values, steps):
    if all(step == steps[0] for step in steps):
        got = send(jnp.concatenate(values, axis=0), *steps[0])
        first = values[0].shape[0]
        return [got[:first], got[first:]]
    return [send(value, *step) for value, step in zip(values, steps)]


def reduce_parts(kept, sent, orders, halvings):
    for number, steps in enumerate(zip(*orders)):
        if number < halvings:
            if number:
                halves = [v.shape[0] // 2 for v in kept]
                sent = [v[h:] for v, h in zip(kept, halves)]
                kept = [v[:h] for v, h in zip(kept, halves)]
            if number == 0:
                got = [send(v, *s) for v, s in zip(sent, steps)]
            else:
                got = exchange(sent, steps)
        else:
            got = exchange(kept, steps)
        kept = [v + g for v, g in zip(kept, got)]
    for number in range(halvings - 1, 0, -1):
        got = exchange(kept, [order[number] for order in orders])
        kept = [jnp.concatenate([v, g], axis=0) for v, g in zip(kept, got)]
    got = [send(v, *order[0]) for v, order in zip(kept, orders)]
    return kept, got


def gram_kernel(chunks, dev_ref, row_ref, keys_ref, s_ref, *refs):
    outs, work = refs[:4], refs[4:]
    tiles = s_ref.shape[1] // TILE
    spots = places(tiles)
    parts = bands_of(tiles)
    pivots = dev_ref.shape[0]
    for part in range(2):
        where = {(i, j): row for i, j, row in spots[part][0]}
        for band in parts[part]:
            first = band * BAND * TILE
            strip = dot(s_ref[:, first:first + BAND * TILE], s_ref[:, first:], 0, 0)
            for a in range(BAND):
                i = band * BAND + a
                for j in range(i, tiles):
                    col = (j - band * BAND) * TILE
                    row = where[(i, j)]
                    work[part][row:row + TILE, :] = strip[
                        a * TILE:(a + 1) * TILE, col:col + TILE]
    base = spots[0][1]
    sub = iota((16, s_ref.shape[1]), 0)

    def pick(p, carry):
        at = row_ref[p]
        group = pl.multiple_of((at // 16) * 16, 16)
        rows = s_ref[pl.ds(group, 16), :].astype(F32)
        wanted = jnp.where(dev_ref[p] == keys_ref[2], at - group, -1)
        row = jnp.sum(jnp.where(sub == wanted, rows, 0.0), axis=0, keepdims=True)
        for t in range(tiles):
            work[0][pl.ds(base + t * pivots + p, 1), :] = row[:, t * TILE:(t + 1) * TILE]
        return carry

    lax.fori_loop(0, pivots, pick, 0)
    for part in range(2):
        size = work[part].shape[0] // chunks
        for q in range(chunks):
            out = outs[2 * part + q // (chunks // 2)]
            to = (q % (chunks // 2)) * size
            at = pl.multiple_of((keys_ref[part] ^ q) * size, 8)
            out[to:to + size, :] = work[part][pl.ds(at, size), :]


def local_gram(snapshots, pivot_dev, pivot_row, keys, rows, chunks):
    shapes = [jax.ShapeDtypeStruct((r // 2, TILE), F32) for r in rows for _ in range(2)]
    return pl.pallas_call(
        functools.partial(gram_kernel, chunks),
        out_shape=shapes,
        in_specs=[SMEM, SMEM, SMEM, VMEM],
        out_specs=[VMEM] * 4,
        scratch_shapes=[pltpu.VMEM((r, TILE), F32) for r in rows],
        name="local_gram",
    )(pivot_dev, pivot_row, keys, snapshots)


def eliminate(rows, at):
    shape = rows[0].shape
    sub = iota(shape, 0)

    def lane(value, j):
        return jnp.broadcast_to(value[:, j:j + 1], shape)

    def subl(value, i):
        return jnp.broadcast_to(value[i:i + 1, :], shape)

    rows = list(rows)
    count = len(rows)
    for g in range(count):
        here = rows[g]
        cols = [lane(here, at + 8 * g + j) for j in range(8)]
        p = [[subl(cols[j], i) if j >= i else None for j in range(8)] for i in range(8)]
        e = [subl(here, i) for i in range(8)]
        below = range(g + 1, count)
        c = {h: [lane(rows[h], at + 8 * g + j) for j in range(8)] for h in below}
        scale = [None] * 8
        for j in range(0, 8, 2):
            k = j + 1
            a, b, d = p[j][j], p[j][k], p[k][k]
            idet = 1.0 / (a * d - b * b)
            ia = 1.0 / a
            scale[j], scale[k] = ia, a * idet
            e[k] = e[k] - (b * ia) * e[j]
            for i in range(j + 2, 8):
                y0 = d * p[j][i] - b * p[k][i]
                y1 = a * p[k][i] - b * p[j][i]
                for m in range(i, 8):
                    p[i][m] = p[i][m] - (y0 * p[j][m] + y1 * p[k][m]) * idet
                e[i] = e[i] - (p[j][i] * ia) * e[j] - (y1 * idet) * e[k]
            for h in below:
                x0 = (d * c[h][j] - b * c[h][k]) * idet
                x1 = (a * c[h][k] - b * c[h][j]) * idet
                for m in range(j + 2, 8):
                    c[h][m] = c[h][m] - x0 * p[j][m] - x1 * p[k][m]
                rows[h] = rows[h] - (c[h][j] * ia) * e[j] - x1 * e[k]
        out, factor = e[0], scale[0]
        for i in range(1, 8):
            out = jnp.where(sub == i, e[i], out)
            factor = jnp.where(sub == i, scale[i], factor)
        rows[g] = out * jnp.sqrt(factor)
    return rows


def lower(value):
    return jnp.where(iota(value.shape, 1) <= iota(value.shape, 0), value, 0.0)


def invert_factor(m_ref):
    n, b = m_ref.shape[0], BLOCK
    lanes, subs = iota((b, n), 1), iota((b, n), 0)
    near, down = iota((b, TILE), 1), iota((b, TILE), 0)
    for k in range(n // b):
        first = k * b
        tile = first // TILE * TILE
        at = first - tile
        other = b - at
        inside = (near >= at) & (near < at + b)
        eye = jnp.where(near - other == down, 1.0, 0.0)
        block = jnp.where(inside, m_ref[first:first + b, tile:tile + TILE], eye)
        done = eliminate([block[8 * g:8 * g + 8] for g in range(b // 8)], at)
        inverse = lower(jnp.concatenate(done, axis=0)[:, other:other + b])
        mine = (lanes >= first) & (lanes < first + b)
        unit = jnp.where(lanes - first == subs, 1.0, 0.0)
        row = dot(inverse, jnp.where(mine, unit, m_ref[first:first + b, :]), 1, 0, HIGHEST)
        m_ref[first:first + b, :] = row
        if first + b < n:
            update = dot(row, row, 0, 0, HIGHEST)
            for q in range(first + b, n, b):
                m_ref[q:q + b, :] = (
                    jnp.where(mine, 0.0, m_ref[q:q + b, :]) - update[q:q + b, :]
                )


def inverse_factor(matrix, m_ref):
    n = matrix.shape[0]
    diagonal = jnp.where(iota((n, n), 0) == iota((n, n), 1), matrix, 0.0)
    down = lax.rsqrt(jnp.sum(diagonal, axis=1, keepdims=True))
    across = lax.rsqrt(jnp.sum(diagonal, axis=0, keepdims=True))
    m_ref[...] = matrix * down * across
    invert_factor(m_ref)
    return lower(m_ref[...]) * across


def solve_kernel(
    chunks, rows_total, keys_ref, start_ref, s_ref, a0_ref, a1_ref, b0_ref, b1_ref,
    modes_ref, scores_ref, basis_ref, pa_ref, pb_ref, gh_ref, gl_ref, xh_ref, xl_ref,
    y_ref, m_ref,
):
    packed = (pa_ref, pb_ref)
    halves = ((a0_ref, a1_ref), (b0_ref, b1_ref))
    snap, rank = start_ref.shape
    tiles = snap // TILE
    for part in range(2):
        size = packed[part].shape[0] // chunks
        for q in range(chunks):
            half = halves[part][q // (chunks // 2)]
            at = (q % (chunks // 2)) * size
            to = pl.multiple_of((keys_ref[part] ^ q) * size, 8)
            packed[part][pl.ds(to, size), :] = half[at:at + size, :]
    spots = places(tiles)
    for part in range(2):
        for i, j, row in spots[part][0]:
            value = packed[part][row:row + TILE, :]
            high, low = split(value)
            gh_ref[i * TILE:(i + 1) * TILE, j * TILE:(j + 1) * TILE] = high
            gl_ref[i * TILE:(i + 1) * TILE, j * TILE:(j + 1) * TILE] = low
            if i != j:
                high, low = split(jnp.transpose(value))
                gh_ref[j * TILE:(j + 1) * TILE, i * TILE:(i + 1) * TILE] = high
                gl_ref[j * TILE:(j + 1) * TILE, i * TILE:(i + 1) * TILE] = low
    xh_ref[...], xl_ref[...] = split(start_ref[...])
    step = 256

    def apply_gram():
        xh, xl = xh_ref[...], xl_ref[...]

        def strip(r, carry):
            at = pl.ds(pl.multiple_of(r * step, step), step)
            gh = gh_ref[at, :]
            y_ref[at, :] = dot(gh, xh, 1, 0) + (dot(gh, xl, 1, 0) + dot(gl_ref[at, :], xh, 1, 0))
            return carry

        lax.fori_loop(0, snap // step, strip, 0)

    def iteration(_, carry):
        apply_gram()
        yh, yl = split(y_ref[...])
        factor = inverse_factor(dot(yh, yh, 0, 0), m_ref).astype(BF16)
        xh_ref[...], xl_ref[...] = split(dot(yh, factor, 1, 1) + dot(yl, factor, 1, 1))
        return carry

    lax.fori_loop(0, ITERS, iteration, 0)
    apply_gram()
    yh, yl = split(y_ref[...])
    xh, xl = xh_ref[...], xl_ref[...]
    small = dot(xh, yh, 0, 0) + (dot(xh, yl, 0, 0) + dot(xl, yh, 0, 0))
    small = (small + jnp.transpose(small)) * (0.5 / rows_total)
    fh, fl = split(inverse_factor(small, m_ref))
    coef = (dot(xh, fh, 1, 1) + (dot(xh, fl, 1, 1) + dot(xl, fh, 1, 1))).astype(BF16)
    xh_ref[...] = coef

    base = spots[0][1]
    pivots = basis_ref.shape[1]
    picked = jnp.concatenate(
        [pa_ref[base + t * pivots:base + (t + 1) * pivots, :] for t in range(tiles)], axis=1
    )
    panel = dot(picked.astype(BF16), coef, 1, 0)
    gram = dot(panel, panel, 1, 1, HIGHEST)
    same = iota((pivots, pivots), 0) == iota((pivots, pivots), 1)
    diagonal = jnp.where(same, gram, 0.0)
    down = lax.rsqrt(jnp.sum(diagonal, axis=1, keepdims=True))
    across = lax.rsqrt(jnp.sum(diagonal, axis=0, keepdims=True))
    wide = jnp.concatenate(
        [gram * down * across, jnp.where(same, 1.0, 0.0)]
        + [jnp.zeros((pivots, TILE - 2 * pivots), F32)], axis=1
    )
    done = eliminate([wide[8 * g:8 * g + 8] for g in range(pivots // 8)], 0)
    factor = lower(jnp.concatenate(done, axis=0)[:, pivots:2 * pivots]) * across
    turned = dot(factor, panel, 1, 0, HIGHEST)
    basis_ref[...] = dot(panel, factor, 0, 1, HIGHEST)
    th, tl = split(turned)
    ones = jnp.ones((8, rank), BF16)
    chunk = 512

    def project(r, carry):
        at = pl.ds(pl.multiple_of(r * chunk, chunk), chunk)
        basis = dot(s_ref[at, :], xh_ref[...], 1, 0)
        bh, bl = split(basis)
        modes_ref[at, :] = bh
        coeffs = dot(bh, th, 1, 1) + (dot(bh, tl, 1, 1) + dot(bl, th, 1, 1))
        ch, cl = split(coeffs)
        left = basis - (dot(ch, th, 1, 0) + (dot(ch, tl, 1, 0) + dot(cl, th, 1, 0)))
        qh, ql = split(left * left)
        total = (dot(ones, qh, 1, 1) + dot(ones, ql, 1, 1)) * (1.0 / rank)
        scores_ref[:, at] = total[0:1, :]
        return carry

    lax.fori_loop(0, s_ref.shape[0] // chunk, project, 0)


def solve(snapshots, start, keys, pieces, pivots, rows, chunks, rows_total):
    snap, rank = start.shape
    here = snapshots.shape[0]
    return pl.pallas_call(
        functools.partial(solve_kernel, chunks, rows_total),
        out_shape=[
            jax.ShapeDtypeStruct((here, rank), BF16),
            jax.ShapeDtypeStruct((1, here), F32),
            jax.ShapeDtypeStruct((rank, pivots), F32),
        ],
        in_specs=[SMEM] + [VMEM] * 6,
        out_specs=[VMEM] * 3,
        scratch_shapes=[pltpu.VMEM((r, TILE), F32) for r in rows] + [
            pltpu.VMEM((snap, snap), BF16),
            pltpu.VMEM((snap, snap), BF16),
            pltpu.VMEM((snap, rank), BF16),
            pltpu.VMEM((snap, rank), BF16),
            pltpu.VMEM((snap, rank), F32),
            pltpu.VMEM((rank, rank), F32),
        ],
        name="solve",
    )(keys, start, snapshots, *pieces)


def local(mesh_shape, snapshots, start, pivot_dev, pivot_row):
    here, snap = snapshots.shape
    pivots = pivot_dev.shape[0]
    spots = places(snap // TILE)
    rows = [spots[0][1] + pivots * (snap // TILE), spots[1][1]]
    orders, halvings = exchange_plan(mesh_shape, rows)
    chunks = 1 << halvings
    myself = lax.axis_index(("grp", "blk"))
    keys = jnp.stack([key_of(orders[0], halvings), key_of(orders[1], halvings), myself])
    a0, a1, b0, b1 = local_gram(snapshots, pivot_dev, pivot_row, keys, rows, chunks)
    own, other = reduce_parts([a0, b0], [a1, b1], orders, halvings)
    pieces = (own[0], other[0], own[1], other[1])
    rows_total = here * mesh_shape["grp"] * mesh_shape["blk"]
    modes, scores, basis = solve(
        snapshots, start, keys, pieces, pivots, rows, chunks, rows_total
    )
    return modes, scores.reshape(here), basis


def solution(mesh):
    placed = (P(("grp", "blk"), None), P(), P(), P())
    return jax.shard_map(
        functools.partial(local, dict(mesh.shape)),
        mesh=mesh,
        in_specs=placed,
        out_specs=(P(("grp", "blk"), None), P(("grp", "blk")), P()),
        check_vma=False,
    )
```

```python
import functools
import jax
import jax.numpy as jnp
from jax import lax
from jax.experimental import pallas as pl
from jax.experimental.pallas import tpu as pltpu
from jax.sharding import PartitionSpec as P


ITERS = 4
TILE = 128
BAND = 2
BLOCK = 64
LOADS = 4
F32, BF16 = jnp.float32, jnp.bfloat16
HIGHEST = lax.Precision.HIGHEST
VMEM = pl.BlockSpec(memory_space=pltpu.VMEM)
SMEM = pl.BlockSpec(memory_space=pltpu.SMEM)
ANY = pl.BlockSpec(memory_space=pl.ANY)


def dot(a, b, ca, cb, precision=None):
    return lax.dot_general(
        a, b, (((ca,), (cb,)), ((), ())), precision=precision, preferred_element_type=F32
    )


def split(value):
    high = value.astype(BF16)
    return high, (value - high.astype(F32)).astype(BF16)


def iota(shape, dim):
    return lax.broadcasted_iota(jnp.int32, shape, dim)


def bands_of(tiles):
    count = tiles // BAND
    outer = [0, count - 1] if count > 1 else [0]
    return outer, [band for band in range(count) if band not in outer]


def places(tiles):
    result = []
    for bands in bands_of(tiles):
        row, entries = 0, []
        for band in bands:
            for i in range(band * BAND, band * BAND + BAND):
                for j in range(i, tiles):
                    entries.append((i, j, row))
                    row += TILE
        result.append((entries, row))
    return result


def exchange_plan(mesh_shape, rows):
    grp = [("grp", 1 << b) for b in range(mesh_shape["grp"].bit_length() - 1)]
    blk = [("blk", 1 << b) for b in range(mesh_shape["blk"].bit_length() - 1)]
    rest = blk[1:] + grp[2:]
    orders = (grp[:1] + blk[:1] + grp[1:2] + rest, grp[:1] + grp[1:2] + blk[:1] + rest)
    halvings = 0
    while halvings < len(orders[0]) and all(r % (8 << (halvings + 1)) == 0 for r in rows):
        halvings += 1
    return orders, halvings


def key_of(order, halvings):
    key = jnp.int32(0)
    for axis, mask in order[:halvings]:
        key = key * 2 + jnp.where((lax.axis_index(axis) & mask) != 0, 1, 0)
    return key


def send(value, axis, mask):
    size = lax.axis_size(axis)
    return lax.ppermute(value, axis, [(i, i ^ mask) for i in range(size)])


def exchange(values, steps):
    if all(step == steps[0] for step in steps):
        got = send(jnp.concatenate(values, axis=0), *steps[0])
        first = values[0].shape[0]
        return [got[:first], got[first:]]
    result = []
    for value, step in zip(values, steps):
        result.append(send(value, *step))
    return result


def halve(values, got):
    halves = [v.shape[0] // 2 for v in values]
    sent = [v[h:] + g[h:] for v, g, h in zip(values, got, halves)]
    kept = [v[:h] + g[:h] for v, g, h in zip(values, got, halves)]
    return sent, kept


def reduce_parts(kept, sent, got, orders, halvings):
    steps = list(zip(*orders))
    for number in range(1, len(steps)):
        if number < halvings:
            sent, kept = halve(kept, got)
            got = exchange(sent, steps[number])
        else:
            kept = [v + g for v, g in zip(kept, got)]
            got = exchange(kept, steps[number])
    kept = [v + g for v, g in zip(kept, got)]
    for number in range(halvings - 1, 0, -1):
        got = exchange(kept, steps[number])
        kept = [jnp.concatenate([v, g], axis=0) for v, g in zip(kept, got)]
    return kept, [send(v, *order[0]) for v, order in zip(kept, orders)]


def gram_kernel(part, chunks, dev_ref, row_ref, keys_ref, s_hbm, low_ref, high_ref, s_ref, work, sems):
    tiles = s_ref.shape[1] // TILE
    spots = places(tiles)
    here = s_ref.shape[0]
    piece = here // LOADS
    copies = []
    for q in range(LOADS):
        at = pl.ds(q * piece, piece)
        copies.append(pltpu.make_async_copy(s_hbm.at[at, :], s_ref.at[at, :], sems.at[q]))
        copies[-1].start()
    where = {(i, j): row for i, j, row in spots[part][0]}
    for q in range(LOADS):
        copies[q].wait()
        rows = slice(q * piece, (q + 1) * piece)
        for band in bands_of(tiles)[part]:
            first = band * BAND * TILE
            strip = dot(s_ref[rows, first:first + BAND * TILE], s_ref[rows, first:], 0, 0)
            for a in range(BAND):
                i = band * BAND + a
                for j in range(i, tiles):
                    col = (j - band * BAND) * TILE
                    row = where[(i, j)]
                    term = strip[a * TILE:(a + 1) * TILE, col:col + TILE]
                    if q:
                        term = work[row:row + TILE, :] + term
                    work[row:row + TILE, :] = term
    if part == 0:
        base = spots[0][1]
        pivots = dev_ref.shape[0]
        sub = iota((16, s_ref.shape[1]), 0)

        def pick(p, carry):
            at = row_ref[p]
            group = pl.multiple_of((at // 16) * 16, 16)
            rows = s_ref[pl.ds(group, 16), :].astype(F32)
            wanted = jnp.where(dev_ref[p] == keys_ref[2], at - group, -1)
            row = jnp.sum(jnp.where(sub == wanted, rows, 0.0), axis=0, keepdims=True)
            for t in range(tiles):
                work[pl.ds(base + t * pivots + p, 1), :] = row[:, t * TILE:(t + 1) * TILE]
            return carry

        lax.fori_loop(0, pivots, pick, 0)
    size = work.shape[0] // chunks
    for q in range(chunks):
        out = low_ref if q < chunks // 2 else high_ref
        to = (q % (chunks // 2)) * size
        at = pl.multiple_of((keys_ref[part] ^ q) * size, 8)
        out[to:to + size, :] = work[pl.ds(at, size), :]


def local_gram(part, snapshots, pivot_dev, pivot_row, keys, rows, chunks):
    here, snap = snapshots.shape
    return pl.pallas_call(
        functools.partial(gram_kernel, part, chunks),
        out_shape=[jax.ShapeDtypeStruct((rows // 2, TILE), F32)] * 2,
        in_specs=[SMEM, SMEM, SMEM, ANY],
        out_specs=[VMEM] * 2,
        scratch_shapes=[
            pltpu.VMEM((here, snap), BF16),
            pltpu.VMEM((rows, TILE), F32),
            pltpu.SemaphoreType.DMA((LOADS,)),
        ],
    )(pivot_dev, pivot_row, keys, snapshots)


def eliminate(rows, at):
    shape = rows[0].shape
    sub = iota(shape, 0)
    one = jnp.where(sub >= 0, 1.0, 0.0)

    def lane(value, j):
        return jnp.broadcast_to(value[:, j:j + 1], shape)

    def subl(value, i):
        return jnp.broadcast_to(value[i:i + 1, :], shape)

    rows = list(rows)
    count = len(rows)
    for g in range(count):
        here = rows[g]
        cols = [lane(here, at + 8 * g + j) * one for j in range(8)]
        p = [[subl(cols[j], i) if j >= i else None for j in range(8)] for i in range(8)]
        e = [subl(here, i) for i in range(8)]
        c = {h: [lane(rows[h], at + 8 * g + j) for j in range(8)] for h in range(g + 1, count)}
        scale = []
        u = [[None] * 8 for _ in range(8)]
        for j in range(8):
            inverse = 1.0 / p[j][j]
            scale.append(inverse)
            for i in range(j + 1, 8):
                u[j][i] = p[j][i] * inverse
            for i in range(j + 1, 8):
                for m in range(i, 8):
                    if i == j + 1 and m <= j + 2:
                        p[i][m] = p[i][m] - (p[j][i] * p[j][m]) * inverse
                    else:
                        p[i][m] = p[i][m] - u[j][i] * p[j][m]
                e[i] = e[i] - u[j][i] * e[j]
            if g + 1 < count:
                near = c[g + 1]
                x = near[j] * inverse
                rows[g + 1] = rows[g + 1] - x * e[j]
                for m in range(j + 1, 8):
                    near[m] = near[m] - x * p[j][m]
        if g + 2 < count:
            t = [e[i] * scale[i] for i in range(8)]
            for i in range(7, 0, -1):
                for m in range(i):
                    t[m] = t[m] - u[m][i] * t[i]
            for h in range(g + 2, count):
                terms = [c[h][j] * t[j] for j in range(8)]
                while len(terms) > 1:
                    terms = [terms[q] + terms[q + 1] for q in range(0, len(terms), 2)]
                rows[h] = rows[h] - terms[0]
        out, factor = e[0], scale[0]
        for i in range(1, 8):
            out = jnp.where(sub == i, e[i], out)
            factor = jnp.where(sub == i, scale[i], factor)
        rows[g] = out * jnp.sqrt(factor)
    return rows


def lower(value):
    return jnp.where(iota(value.shape, 1) <= iota(value.shape, 0), value, 0.0)


def invert_factor(m_ref, beside=None):
    n, b = m_ref.shape[0], BLOCK
    lanes, subs = iota((b, n), 1), iota((b, n), 0)
    near, down = iota((b, TILE), 1), iota((b, TILE), 0)
    block = m_ref[:b, :TILE]
    for k in range(n // b):
        first = k * b
        at = first % TILE
        other = b - at
        inside = (near >= at) & (near < at + b)
        eye = jnp.where(near - other == down, 1.0, 0.0)
        block = jnp.where(inside, block, eye)
        if beside is not None:
            beside(k)
        done = eliminate([block[8 * g:8 * g + 8] for g in range(b // 8)], at)
        inverse = lower(jnp.concatenate(done, axis=0)[:, other:other + b])
        mine = (lanes >= first) & (lanes < first + b)
        unit = jnp.where(lanes - first == subs, 1.0, 0.0)
        wh, wl = split(inverse)
        rh, rl = split(jnp.where(mine, unit, m_ref[first:first + b, :]))
        row = dot(wh, rh, 1, 0) + (dot(wh, rl, 1, 0) + dot(wl, rh, 1, 0))
        m_ref[first:first + b, :] = row
        q = first + b
        if q < n:
            uh, ul = split(row)
            left = jnp.concatenate([uh, uh, ul], axis=0)
            right = jnp.concatenate([uh, ul, uh], axis=0)
            tile = q // TILE * TILE
            block = m_ref[q:q + b, tile:tile + TILE] - dot(
                left[:, q:q + b], right[:, tile:tile + TILE], 0, 0)
            update = dot(left, right, 0, 0)
            for q in range(first + b, n, b):
                m_ref[q:q + b, :] = (
                    jnp.where(mine, 0.0, m_ref[q:q + b, :]) - update[q:q + b, :]
                )


def inverse_factor(matrix, m_ref, beside=None):
    n = matrix.shape[0]
    diagonal = jnp.where(iota((n, n), 0) == iota((n, n), 1), matrix, 0.0)
    down = lax.rsqrt(jnp.sum(diagonal, axis=1, keepdims=True))
    across = lax.rsqrt(jnp.sum(diagonal, axis=0, keepdims=True))
    m_ref[...] = matrix * down * across
    invert_factor(m_ref, beside)
    return lower(m_ref[...]) * across


def solve_kernel(
    chunks, rows_total, keys_ref, start_ref, s_hbm, a0_ref, a1_ref, b0_ref, b1_ref,
    modes_ref, scores_ref, basis_ref, pa_ref, pb_ref, gh_ref, gl_ref, xh_ref, xl_ref,
    yh_ref, yl_ref, z_ref, m_ref, s_ref, sem,
):
    load = pltpu.make_async_copy(s_hbm, s_ref, sem)
    load.start()
    packed = (pa_ref, pb_ref)
    halves = ((a0_ref, a1_ref), (b0_ref, b1_ref))
    snap, rank = start_ref.shape
    tiles = snap // TILE
    for part in range(2):
        size = packed[part].shape[0] // chunks
        for q in range(chunks):
            half = halves[part][q // (chunks // 2)]
            at = (q % (chunks // 2)) * size
            to = pl.multiple_of((keys_ref[part] ^ q) * size, 8)
            packed[part][pl.ds(to, size), :] = half[at:at + size, :]
    spots = places(tiles)
    for part in range(2):
        for i, j, row in spots[part][0]:
            value = packed[part][row:row + TILE, :]
            high, low = split(value)
            gh_ref[i * TILE:(i + 1) * TILE, j * TILE:(j + 1) * TILE] = high
            gl_ref[i * TILE:(i + 1) * TILE, j * TILE:(j + 1) * TILE] = low
            if i != j:
                high, low = split(jnp.transpose(value))
                gh_ref[j * TILE:(j + 1) * TILE, i * TILE:(i + 1) * TILE] = high
                gl_ref[j * TILE:(j + 1) * TILE, i * TILE:(i + 1) * TILE] = low
    strips = rank // BLOCK
    step = snap // strips

    def product(at, xh, xl):
        gh = gh_ref[at, :]
        return dot(gh, xh, 1, 0) + (dot(gh, xl, 1, 0) + dot(gl_ref[at, :], xh, 1, 0))

    yh_ref[...], yl_ref[...] = split(start_ref[...])
    for r in range(strips):
        at = pl.ds(r * step, step)
        z_ref[at, :] = product(at, yh_ref[...], yl_ref[...])
    yh_ref[...], yl_ref[...] = split(z_ref[...])

    def iteration(number, carry):
        def beside(k):
            at = pl.ds(k * step, step)
            z_ref[at, :] = product(at, yh_ref[...], yl_ref[...])

        yh = yh_ref[...]
        factor = inverse_factor(dot(yh, yh, 0, 0), m_ref, beside).astype(BF16)

        @pl.when(number == ITERS - 1)
        def _():
            iterate = dot(yh_ref[...], factor, 1, 1) + dot(yl_ref[...], factor, 1, 1)
            xh_ref[...], xl_ref[...] = split(iterate)

        zh, zl = split(z_ref[...])
        yh_ref[...], yl_ref[...] = split(dot(zh, factor, 1, 1) + dot(zl, factor, 1, 1))
        return carry

    lax.fori_loop(0, ITERS, iteration, 0)
    yh, yl = yh_ref[...], yl_ref[...]
    xh, xl = xh_ref[...], xl_ref[...]
    small = dot(xh, yh, 0, 0) + (dot(xh, yl, 0, 0) + dot(xl, yh, 0, 0))
    small = (small + jnp.transpose(small)) * (0.5 / rows_total)
    fh, fl = split(inverse_factor(small, m_ref))
    coef = (dot(xh, fh, 1, 1) + (dot(xh, fl, 1, 1) + dot(xl, fh, 1, 1))).astype(BF16)
    xh_ref[...] = coef

    base = spots[0][1]
    pivots = basis_ref.shape[1]
    picked = jnp.concatenate(
        [pa_ref[base + t * pivots:base + (t + 1) * pivots, :] for t in range(tiles)], axis=1
    )
    panel = dot(picked.astype(BF16), coef, 1, 0)
    gram = dot(panel, panel, 1, 1, HIGHEST)
    same = iota((pivots, pivots), 0) == iota((pivots, pivots), 1)
    diagonal = jnp.where(same, gram, 0.0)
    down = lax.rsqrt(jnp.sum(diagonal, axis=1, keepdims=True))
    across = lax.rsqrt(jnp.sum(diagonal, axis=0, keepdims=True))
    wide = jnp.concatenate(
        [gram * down * across, jnp.where(same, 1.0, 0.0)]
        + [jnp.zeros((pivots, TILE - 2 * pivots), F32)], axis=1
    )
    done = eliminate([wide[8 * g:8 * g + 8] for g in range(pivots // 8)], 0)
    factor = lower(jnp.concatenate(done, axis=0)[:, pivots:2 * pivots]) * across
    turned = dot(factor, panel, 1, 0, HIGHEST)
    basis_ref[...] = dot(panel, factor, 0, 1, HIGHEST)
    th, tl = split(turned)
    ones = jnp.ones((8, rank), BF16)
    chunk = 512
    load.wait()

    def project(r, carry):
        at = pl.ds(pl.multiple_of(r * chunk, chunk), chunk)
        basis = dot(s_ref[at, :], xh_ref[...], 1, 0)
        bh, bl = split(basis)
        modes_ref[at, :] = bh
        coeffs = dot(bh, th, 1, 1) + (dot(bh, tl, 1, 1) + dot(bl, th, 1, 1))
        ch, cl = split(coeffs)
        left = basis - (dot(ch, th, 1, 0) + (dot(ch, tl, 1, 0) + dot(cl, th, 1, 0)))
        qh, ql = split(left * left)
        total = (dot(ones, qh, 1, 1) + dot(ones, ql, 1, 1)) * (1.0 / rank)
        scores_ref[:, at] = total[0:1, :]
        return carry

    lax.fori_loop(0, s_ref.shape[0] // chunk, project, 0)


def solve(snapshots, start, keys, pieces, pivots, rows, chunks, rows_total):
    snap, rank = start.shape
    here = snapshots.shape[0]
    return pl.pallas_call(
        functools.partial(solve_kernel, chunks, rows_total),
        out_shape=[
            jax.ShapeDtypeStruct((here, rank), BF16),
            jax.ShapeDtypeStruct((1, here), F32),
            jax.ShapeDtypeStruct((rank, pivots), F32),
        ],
        in_specs=[SMEM, VMEM, ANY] + [VMEM] * 4,
        out_specs=[VMEM] * 3,
        scratch_shapes=[pltpu.VMEM((r, TILE), F32) for r in rows] + [
            pltpu.VMEM((snap, snap), BF16),
            pltpu.VMEM((snap, snap), BF16),
            pltpu.VMEM((snap, rank), BF16),
            pltpu.VMEM((snap, rank), BF16),
            pltpu.VMEM((snap, rank), BF16),
            pltpu.VMEM((snap, rank), BF16),
            pltpu.VMEM((snap, rank), F32),
            pltpu.VMEM((rank, rank), F32),
            pltpu.VMEM((here, snap), BF16),
            pltpu.SemaphoreType.DMA,
        ],
        name="solve",
    )(keys, start, snapshots, *pieces)


def local(mesh_shape, snapshots, start, pivot_dev, pivot_row):
    here, snap = snapshots.shape
    pivots = pivot_dev.shape[0]
    spots = places(snap // TILE)
    rows = [spots[0][1] + pivots * (snap // TILE), spots[1][1]]
    orders, halvings = exchange_plan(mesh_shape, rows)
    chunks = 1 << halvings
    myself = lax.axis_index(("grp", "blk"))
    keys = jnp.stack([key_of(orders[0], halvings), key_of(orders[1], halvings), myself])
    first = [order[0] for order in orders]
    a0, a1 = local_gram(0, snapshots, pivot_dev, pivot_row, keys, rows[0], chunks)
    got_a = send(a1, *first[0])
    b0, b1 = local_gram(1, snapshots, pivot_dev, pivot_row, keys, rows[1], chunks)
    got = [got_a, send(b1, *first[1])]
    own, other = reduce_parts([a0, b0], [a1, b1], got, orders, halvings)
    pieces = (own[0], other[0], own[1], other[1])
    rows_total = here * mesh_shape["grp"] * mesh_shape["blk"]
    modes, scores, basis = solve(
        snapshots, start, keys, pieces, pivots, rows, chunks, rows_total
    )
    return modes, scores.reshape(here), basis


def solution(mesh):
    placed = (P(("grp", "blk"), None), P(), P(), P())

    def body(*args):
        return local(dict(mesh.shape), *args)

    return jax.shard_map(
        body,
        mesh=mesh,
        in_specs=placed,
        out_specs=(P(("grp", "blk"), None), P(("grp", "blk")), P()),
        check_vma=False,
    )
```

```python
import functools
import jax
import jax.numpy as jnp
from jax import lax
from jax.experimental import pallas as pl
from jax.experimental.pallas import tpu as pltpu
from jax.sharding import PartitionSpec as P

ITERS = 4
TILE = 128
BAND = 2
BLOCK = 64
LOADS = 2
GRANT = 28 << 20
F32, BF16 = jnp.float32, jnp.bfloat16
HIGHEST = lax.Precision.HIGHEST
VMEM = pl.BlockSpec(memory_space=pltpu.VMEM)
SMEM = pl.BlockSpec(memory_space=pltpu.SMEM)
HBM = pl.BlockSpec(memory_space=pltpu.HBM)


def dot(a, b, ca, cb, precision=None):
    return lax.dot_general(
        a, b, (((ca,), (cb,)), ((), ())), precision=precision, preferred_element_type=F32
    )


def split(value):
    high = value.astype(BF16)
    return high, (value - high.astype(F32)).astype(BF16)


def in_hbm(value):
    return pltpu.with_memory_space_constraint(value, pltpu.HBM)


def iota(shape, dim):
    return lax.broadcasted_iota(jnp.int32, shape, dim)


def bands_of(tiles):
    count = tiles // BAND
    outer = [0, count - 1] if count > 1 else [0]
    return outer, [band for band in range(count) if band not in outer]


def places(tiles):
    result = []
    for bands in bands_of(tiles):
        row, entries = 0, []
        for band in bands:
            for i in range(band * BAND, band * BAND + BAND):
                for j in range(i, tiles):
                    entries.append((i, j, row))
                    row += TILE
        result.append((entries, row))
    return result


def exchange_plan(mesh_shape, rows):
    grp = [("grp", (1 << b,)) for b in range(mesh_shape["grp"].bit_length() - 1)]
    blk = [("blk", (1 << b,)) for b in range(mesh_shape["blk"].bit_length() - 1)]
    pair = [("blk", blk[1][1] + blk[2][1])] if len(blk) > 2 else blk[1:2]
    rest = pair + blk[3:] + grp[2:]
    orders = (grp[:1] + blk[:1] + grp[1:2] + rest, grp[:1] + grp[1:2] + blk[:1] + rest)
    halvings, ways = 0, 1
    for _, masks in orders[0]:
        ways *= 1 << len(masks)
        if any(r % (8 * ways) for r in rows):
            break
        halvings += 1
    return orders, halvings


def chunks_of(order, halvings):
    return 1 << sum(len(masks) for _, masks in order[:halvings])


def key_of(order, halvings):
    key = jnp.int32(0)
    for axis, masks in order[:halvings]:
        for mask in masks:
            key = key * 2 + jnp.where((lax.axis_index(axis) & mask) != 0, 1, 0)
    return key


def partners(masks):
    result = [0]
    for mask in masks:
        result = [m ^ extra for m in result for extra in (0, mask)]
    return result


def send(value, axis, mask):
    size = lax.axis_size(axis)
    return lax.ppermute(value, axis, [(i, i ^ mask) for i in range(size)])


def exchange(values, stages, mask_at):
    if all(stage == stages[0] for stage in stages):
        axis, masks = stages[0]
        got = send(jnp.concatenate(values, axis=0), axis, partners(masks)[mask_at])
        first = values[0].shape[0]
        return [got[:first], got[first:]]
    return [
        send(value, axis, partners(masks)[mask_at])
        for value, (axis, masks) in zip(values, stages)
    ]


def add_up(terms):
    while len(terms) > 1:
        terms = [a + b for a, b in zip(terms[::2], terms[1::2])]
    return terms[0]


def reduce_parts(kept, sent, orders, halvings):
    stages = list(zip(*orders))
    terms = [[v, send(s, order[0][0], order[0][1][0])] for v, s, order in zip(kept, sent, orders)]
    for number in range(1, len(stages)):
        stage = stages[number]
        count = 1 << len(stage[0][1])
        if number < halvings:
            sizes = [t[0].shape[0] // count for t in terms]
            cut = [
                [add_up([v[q * size:(q + 1) * size] for v in t]) for q in range(count)]
                for t, size in zip(terms, sizes)
            ]
            got = [exchange([c[q] for c in cut], stage, q) for q in range(1, count)]
            terms = [[c[0]] + [g[part] for g in got] for part, c in enumerate(cut)]
        else:
            whole = [add_up(t) for t in terms]
            got = [exchange(whole, stage, q) for q in range(1, count)]
            terms = [[v] + [g[part] for g in got] for part, v in enumerate(whole)]
    kept = [add_up(t) for t in terms]
    for number in range(halvings - 1, 0, -1):
        stage = stages[number]
        got = [exchange(kept, stage, q) for q in range(1, 1 << len(stage[0][1]))]
        kept = [
            jnp.concatenate([v] + [g[part] for g in got], axis=0)
            for part, v in enumerate(kept)
        ]
    return kept, [send(v, order[0][0], order[0][1][0]) for v, order in zip(kept, orders)]


def gram_kernel(chunks, dev_ref, row_ref, keys_ref, s_hbm, *refs):
    outs, work, s_ref, sems = refs[:4], refs[4:6], refs[6], refs[7]
    tiles = s_ref.shape[1] // TILE
    spots = places(tiles)
    piece = s_ref.shape[0] // LOADS
    copies = []
    for q in range(LOADS):
        at = pl.ds(q * piece, piece)
        copies.append(pltpu.make_async_copy(s_hbm.at[at, :], s_ref.at[at, :], sems.at[q]))
        copies[-1].start()
    for q in range(LOADS):
        copies[q].wait()
        rows = slice(q * piece, (q + 1) * piece)
        for part in range(2):
            where = {(i, j): row for i, j, row in spots[part][0]}
            for band in bands_of(tiles)[part]:
                first = band * BAND * TILE
                strip = dot(s_ref[rows, first:first + BAND * TILE], s_ref[rows, first:], 0, 0)
                for a in range(BAND):
                    i = band * BAND + a
                    for j in range(i, tiles):
                        col = (j - band * BAND) * TILE
                        row = where[(i, j)]
                        term = strip[a * TILE:(a + 1) * TILE, col:col + TILE]
                        if q:
                            term = work[part][row:row + TILE, :] + term
                        work[part][row:row + TILE, :] = term
    base = spots[0][1]
    pivots = dev_ref.shape[0]
    sub = iota((16, s_ref.shape[1]), 0)

    def pick(p, carry):
        at = row_ref[p]
        group = pl.multiple_of((at // 16) * 16, 16)
        rows = s_ref[pl.ds(group, 16), :].astype(F32)
        wanted = jnp.where(dev_ref[p] == keys_ref[2], at - group, -1)
        row = jnp.sum(jnp.where(sub == wanted, rows, 0.0), axis=0, keepdims=True)
        for t in range(tiles):
            work[0][pl.ds(base + t * pivots + p, 1), :] = row[:, t * TILE:(t + 1) * TILE]
        return carry

    lax.fori_loop(0, pivots, pick, 0, unroll=4)
    for part in range(2):
        size = work[part].shape[0] // chunks
        for q in range(chunks):
            out = outs[2 * part + q // (chunks // 2)]
            to = (q % (chunks // 2)) * size
            at = pl.multiple_of((keys_ref[part] ^ q) * size, 8)
            out[to:to + size, :] = work[part][pl.ds(at, size), :]


def local_gram(snapshots, pivot_dev, pivot_row, keys, rows, chunks):
    shapes = [jax.ShapeDtypeStruct((r // 2, TILE), F32) for r in rows for _ in range(2)]
    return pl.pallas_call(
        functools.partial(gram_kernel, chunks),
        out_shape=shapes,
        in_specs=[SMEM, SMEM, SMEM, HBM],
        out_specs=[VMEM] * 4,
        scratch_shapes=[pltpu.VMEM((r, TILE), F32) for r in rows] + [
            pltpu.VMEM(snapshots.shape, BF16),
            pltpu.SemaphoreType.DMA((LOADS,)),
        ],
        compiler_params=pltpu.CompilerParams(vmem_limit_bytes=GRANT),
        name="local_gram",
    )(in_hbm(pivot_dev), in_hbm(pivot_row), keys, in_hbm(snapshots))


def eliminate(rows, at):
    shape = rows[0].shape
    sub = iota(shape, 0)
    one = jnp.where(sub >= 0, 1.0, 0.0)

    def lane(value, j):
        return jnp.broadcast_to(value[:, j:j + 1], shape)

    def subl(value, i):
        return jnp.broadcast_to(value[i:i + 1, :], shape)

    rows = list(rows)
    count = len(rows)
    for g in range(count):
        here = rows[g]
        cols = [lane(here, at + 8 * g + j) * one for j in range(8)]
        p = [[subl(cols[j], i) if j >= i else None for j in range(8)] for i in range(8)]
        e = [subl(here, i) for i in range(8)]
        c = {h: [lane(rows[h], at + 8 * g + j) for j in range(8)] for h in range(g + 1, count)}
        scale = []
        u = [[None] * 8 for _ in range(8)]
        for j in range(8):
            inverse = 1.0 / p[j][j]
            scale.append(inverse)
            for i in range(j + 1, 8):
                u[j][i] = p[j][i] * inverse
            for i in range(j + 1, 8):
                for m in range(i, 8):
                    if i == j + 1 and m <= j + 2:
                        p[i][m] = p[i][m] - (p[j][i] * p[j][m]) * inverse
                    else:
                        p[i][m] = p[i][m] - u[j][i] * p[j][m]
                e[i] = e[i] - u[j][i] * e[j]
            if g + 1 < count:
                near = c[g + 1]
                x = near[j] * inverse
                rows[g + 1] = rows[g + 1] - x * e[j]
                for m in range(j + 1, 8):
                    near[m] = near[m] - x * p[j][m]
        if g + 2 < count:
            t = [e[i] * scale[i] for i in range(8)]
            for i in range(7, 0, -1):
                for m in range(i):
                    t[m] = t[m] - u[m][i] * t[i]
            for h in range(g + 2, count):
                terms = [c[h][j] * t[j] for j in range(8)]
                while len(terms) > 1:
                    terms = [terms[q] + terms[q + 1] for q in range(0, len(terms), 2)]
                rows[h] = rows[h] - terms[0]
        out, factor = e[0], scale[0]
        for i in range(1, 8):
            out = jnp.where(sub == i, e[i], out)
            factor = jnp.where(sub == i, scale[i], factor)
        rows[g] = out * jnp.sqrt(factor)
    return rows


def lower(value):
    return jnp.where(iota(value.shape, 1) <= iota(value.shape, 0), value, 0.0)


def invert_factor(m_ref, beside=None):
    n, b = m_ref.shape[0], BLOCK
    lanes, subs = iota((b, n), 1), iota((b, n), 0)
    near, down = iota((b, TILE), 1), iota((b, TILE), 0)
    block = m_ref[:b, :TILE]
    for k in range(n // b):
        first = k * b
        at = first % TILE
        other = b - at
        inside = (near >= at) & (near < at + b)
        eye = jnp.where(near - other == down, 1.0, 0.0)
        block = jnp.where(inside, block, eye)
        if beside is not None:
            beside(k)
        done = eliminate([block[8 * g:8 * g + 8] for g in range(b // 8)], at)
        inverse = lower(jnp.concatenate(done, axis=0)[:, other:other + b])
        mine = (lanes >= first) & (lanes < first + b)
        unit = jnp.where(lanes - first == subs, 1.0, 0.0)
        wh, wl = split(inverse)
        rh, rl = split(jnp.where(mine, unit, m_ref[first:first + b, :]))
        row = dot(wh, rh, 1, 0) + (dot(wh, rl, 1, 0) + dot(wl, rh, 1, 0))
        m_ref[first:first + b, :] = row
        q = first + b
        if q < n:
            uh, ul = split(row)
            left = jnp.concatenate([uh, uh, ul], axis=0)
            right = jnp.concatenate([uh, ul, uh], axis=0)
            tile = q // TILE * TILE
            block = m_ref[q:q + b, tile:tile + TILE] - dot(
                left[:, q:q + b], right[:, tile:tile + TILE], 0, 0)
            update = dot(left, right, 0, 0)
            for q in range(first + b, n, b):
                m_ref[q:q + b, :] = (
                    jnp.where(mine, 0.0, m_ref[q:q + b, :]) - update[q:q + b, :]
                )


def inverse_factor(matrix, m_ref, beside=None):
    n = matrix.shape[0]
    diagonal = jnp.where(iota((n, n), 0) == iota((n, n), 1), matrix, 0.0)
    down = lax.rsqrt(jnp.sum(diagonal, axis=1, keepdims=True))
    across = lax.rsqrt(jnp.sum(diagonal, axis=0, keepdims=True))
    m_ref[...] = matrix * down * across
    invert_factor(m_ref, beside)
    return lower(m_ref[...]) * across


def solve_kernel(
    chunks, rows_total, keys_ref, start_ref, s_ref, a0_ref, a1_ref, b0_ref, b1_ref,
    modes_ref, scores_ref, basis_ref, pa_ref, pb_ref, gh_ref, gl_ref, xh_ref, xl_ref,
    yh_ref, yl_ref, z_ref, m_ref,
):
    packed = (pa_ref, pb_ref)
    halves = ((a0_ref, a1_ref), (b0_ref, b1_ref))
    snap, rank = start_ref.shape
    tiles = snap // TILE
    for part in range(2):
        size = packed[part].shape[0] // chunks
        for q in range(chunks):
            half = halves[part][q // (chunks // 2)]
            at = (q % (chunks // 2)) * size
            to = pl.multiple_of((keys_ref[part] ^ q) * size, 8)
            packed[part][pl.ds(to, size), :] = half[at:at + size, :]
    spots = places(tiles)
    for part in range(2):
        for i, j, row in spots[part][0]:
            value = packed[part][row:row + TILE, :]
            high, low = split(value)
            gh_ref[i * TILE:(i + 1) * TILE, j * TILE:(j + 1) * TILE] = high
            gl_ref[i * TILE:(i + 1) * TILE, j * TILE:(j + 1) * TILE] = low
            if i != j:
                high, low = split(jnp.transpose(value))
                gh_ref[j * TILE:(j + 1) * TILE, i * TILE:(i + 1) * TILE] = high
                gl_ref[j * TILE:(j + 1) * TILE, i * TILE:(i + 1) * TILE] = low
    strips = rank // BLOCK
    step = snap // strips

    def product(at, xh, xl):
        gh = gh_ref[at, :]
        return dot(gh, xh, 1, 0) + (dot(gh, xl, 1, 0) + dot(gl_ref[at, :], xh, 1, 0))

    yh_ref[...], yl_ref[...] = split(start_ref[...])
    for r in range(strips):
        at = pl.ds(r * step, step)
        z_ref[at, :] = product(at, yh_ref[...], yl_ref[...])
    yh_ref[...], yl_ref[...] = split(z_ref[...])

    def iteration(number, carry):
        def beside(k):
            at = pl.ds(k * step, step)
            z_ref[at, :] = product(at, yh_ref[...], yl_ref[...])

        yh = yh_ref[...]
        factor = inverse_factor(dot(yh, yh, 0, 0), m_ref, beside).astype(BF16)

        @pl.when(number == ITERS - 1)
        def _():
            iterate = dot(yh_ref[...], factor, 1, 1) + dot(yl_ref[...], factor, 1, 1)
            xh_ref[...], xl_ref[...] = split(iterate)

        zh, zl = split(z_ref[...])
        yh_ref[...], yl_ref[...] = split(dot(zh, factor, 1, 1) + dot(zl, factor, 1, 1))
        return carry

    lax.fori_loop(0, ITERS, iteration, 0)
    yh, yl = yh_ref[...], yl_ref[...]
    xh, xl = xh_ref[...], xl_ref[...]
    small = dot(xh, yh, 0, 0) + (dot(xh, yl, 0, 0) + dot(xl, yh, 0, 0))
    small = (small + jnp.transpose(small)) * (0.5 / rows_total)
    fh, fl = split(inverse_factor(small, m_ref))
    coef = (dot(xh, fh, 1, 1) + (dot(xh, fl, 1, 1) + dot(xl, fh, 1, 1))).astype(BF16)
    xh_ref[...] = coef

    chunk = 512
    base = spots[0][1]
    pivots = basis_ref.shape[0]
    picked = jnp.concatenate(
        [pa_ref[base + t * pivots:base + (t + 1) * pivots, :] for t in range(tiles)], axis=1
    )
    panel = dot(picked.astype(BF16), coef, 1, 0)
    gram = dot(panel, panel, 1, 1, HIGHEST)
    same = iota((pivots, pivots), 0) == iota((pivots, pivots), 1)
    diagonal = jnp.where(same, gram, 0.0)
    down = lax.rsqrt(jnp.sum(diagonal, axis=1, keepdims=True))
    across = lax.rsqrt(jnp.sum(diagonal, axis=0, keepdims=True))
    wide = jnp.concatenate(
        [gram * down * across, jnp.where(same, 1.0, 0.0)]
        + [jnp.zeros((pivots, TILE - 2 * pivots), F32)], axis=1
    )
    done = eliminate([wide[8 * g:8 * g + 8] for g in range(pivots // 8)], 0)
    factor = lower(jnp.concatenate(done, axis=0)[:, pivots:2 * pivots]) * across
    turned = dot(factor, panel, 1, 0, HIGHEST)
    basis_ref[...] = turned
    th, tl = split(turned)
    thrice_h = jnp.concatenate([th, th, th], axis=0)
    thrice_l = jnp.concatenate([tl, tl, tl], axis=0)
    stacked = jnp.concatenate([th, tl, th], axis=0)
    from_low = iota((chunk, 3 * pivots), 1) >= 2 * pivots
    ones = jnp.ones((8, rank), BF16)
    def project(r, carry):
        at = pl.ds(pl.multiple_of(r * chunk, chunk), chunk)
        basis = dot(s_ref[at, :], xh_ref[...], 1, 0)
        high = basis.astype(BF16)
        modes_ref[at, :] = high
        coeffs = dot(high, thrice_h, 1, 1) + dot(high, thrice_l, 1, 1)
        ch, cl = split(coeffs)
        left = basis - dot(jnp.where(from_low, cl, ch), stacked, 1, 0)
        qh, ql = split(left * left)
        total = (dot(ones, qh, 1, 1) + dot(ones, ql, 1, 1)) * (1.0 / rank)
        scores_ref[:, at] = total[0:1, :]
        return carry

    lax.fori_loop(0, s_ref.shape[0] // chunk, project, 0, unroll=2)


def solve(snapshots, start, keys, pieces, pivots, rows, chunks, rows_total):
    snap, rank = start.shape
    here = snapshots.shape[0]
    return pl.pallas_call(
        functools.partial(solve_kernel, chunks, rows_total),
        out_shape=[
            jax.ShapeDtypeStruct((here, rank), BF16),
            jax.ShapeDtypeStruct((1, here), F32),
            jax.ShapeDtypeStruct((pivots, rank), F32),
        ],
        in_specs=[SMEM] + [VMEM] * 6,
        out_specs=[VMEM] * 3,
        scratch_shapes=[pltpu.VMEM((r, TILE), F32) for r in rows] + [
            pltpu.VMEM((snap, snap), BF16),
            pltpu.VMEM((snap, snap), BF16),
            pltpu.VMEM((snap, rank), BF16),
            pltpu.VMEM((snap, rank), BF16),
            pltpu.VMEM((snap, rank), BF16),
            pltpu.VMEM((snap, rank), BF16),
            pltpu.VMEM((snap, rank), F32),
            pltpu.VMEM((rank, rank), F32),
        ],
        compiler_params=pltpu.CompilerParams(vmem_limit_bytes=GRANT),
        name="solve",
    )(keys, start, snapshots, *pieces)


def local(mesh_shape, snapshots, start, pivot_dev, pivot_row):
    here, snap = snapshots.shape
    pivots = pivot_dev.shape[0]
    spots = places(snap // TILE)
    rows = [spots[0][1] + pivots * (snap // TILE), spots[1][1]]
    orders, halvings = exchange_plan(mesh_shape, rows)
    chunks = chunks_of(orders[0], halvings)
    myself = lax.axis_index(("grp", "blk"))
    keys = jnp.stack([key_of(orders[0], halvings), key_of(orders[1], halvings), myself])
    a0, a1, b0, b1 = local_gram(snapshots, pivot_dev, pivot_row, keys, rows, chunks)
    own, other = reduce_parts([a0, b0], [a1, b1], orders, halvings)
    pieces = (own[0], other[0], own[1], other[1])
    rows_total = here * mesh_shape["grp"] * mesh_shape["blk"]
    modes, scores, basis = solve(
        snapshots, start, keys, pieces, pivots, rows, chunks, rows_total
    )
    return modes, scores.reshape(here), basis.T


def solution(mesh):
    placed = (P(("grp", "blk"), None), P(), P(), P())
    return jax.shard_map(
        functools.partial(local, dict(mesh.shape)),
        mesh=mesh,
        in_specs=placed,
        out_specs=(P(("grp", "blk"), None), P(("grp", "blk")), P()),
        check_vma=False,
    )
```

```python
import functools
import jax
import jax.numpy as jnp
from jax import lax
from jax.experimental import pallas as pl
from jax.experimental.pallas import tpu as pltpu
from jax.sharding import PartitionSpec as P

ITERS = 4
TILE = 128
BAND = 2
BLOCK = 64
LOADS = 2
GRANT = 28 << 20
F32, BF16 = jnp.float32, jnp.bfloat16
HIGHEST = lax.Precision.HIGHEST
VMEM = pl.BlockSpec(memory_space=pltpu.VMEM)
SMEM = pl.BlockSpec(memory_space=pltpu.SMEM)
HBM = pl.BlockSpec(memory_space=pltpu.HBM)


def dot(a, b, ca, cb, precision=None):
    return lax.dot_general(
        a, b, (((ca,), (cb,)), ((), ())), precision=precision, preferred_element_type=F32
    )


def split(value):
    high = value.astype(BF16)
    return high, (value - high.astype(F32)).astype(BF16)


def in_hbm(value):
    return pltpu.with_memory_space_constraint(value, pltpu.HBM)


def iota(shape, dim):
    return lax.broadcasted_iota(jnp.int32, shape, dim)


def bands_of(tiles):
    count = tiles // BAND
    outer = [0, count - 1] if count > 1 else [0]
    return outer, [band for band in range(count) if band not in outer]


def places(tiles):
    result = []
    for bands in bands_of(tiles):
        row, entries = 0, []
        for band in bands:
            for i in range(band * BAND, band * BAND + BAND):
                for j in range(i, tiles):
                    entries.append((i, j, row))
                    row += TILE
        result.append((entries, row))
    return result


def exchange_plan(mesh_shape, rows):
    grp = [("grp", (1 << b,)) for b in range(mesh_shape["grp"].bit_length() - 1)]
    blk = [("blk", (1 << b,)) for b in range(mesh_shape["blk"].bit_length() - 1)]
    pair = [("blk", blk[1][1] + blk[2][1])] if len(blk) > 2 else blk[1:2]
    rest = pair + blk[3:] + grp[2:]
    orders = (grp[:1] + blk[:1] + grp[1:2] + rest, grp[:1] + grp[1:2] + blk[:1] + rest)
    halvings, ways = 0, 1
    for _, masks in orders[0]:
        ways *= 1 << len(masks)
        if any(r % (8 * ways) for r in rows):
            break
        halvings += 1
    return orders, halvings


def chunks_of(order, halvings):
    return 1 << sum(len(masks) for _, masks in order[:halvings])


def key_of(order, halvings):
    key = jnp.int32(0)
    for axis, masks in order[:halvings]:
        for mask in masks:
            key = key * 2 + jnp.where((lax.axis_index(axis) & mask) != 0, 1, 0)
    return key


def partners(masks):
    result = [0]
    for mask in masks:
        result = [m ^ extra for m in result for extra in (0, mask)]
    return result


def send(value, axis, mask):
    size = lax.axis_size(axis)
    return lax.ppermute(value, axis, [(i, i ^ mask) for i in range(size)])


def exchange(values, stages, mask_at):
    if all(stage == stages[0] for stage in stages):
        axis, masks = stages[0]
        got = send(jnp.concatenate(values, axis=0), axis, partners(masks)[mask_at])
        first = values[0].shape[0]
        return [got[:first], got[first:]]
    return [
        send(value, axis, partners(masks)[mask_at])
        for value, (axis, masks) in zip(values, stages)
    ]


def add_up(terms):
    while len(terms) > 1:
        terms = [a + b for a, b in zip(terms[::2], terms[1::2])]
    return terms[0]


def reduce_parts(kept, sent, orders, halvings):
    stages = list(zip(*orders))
    terms = [[v, send(s, order[0][0], order[0][1][0])] for v, s, order in zip(kept, sent, orders)]
    for number in range(1, len(stages)):
        stage = stages[number]
        count = 1 << len(stage[0][1])
        if number < halvings:
            sizes = [t[0].shape[0] // count for t in terms]
            cut = [
                [add_up([v[q * size:(q + 1) * size] for v in t]) for q in range(count)]
                for t, size in zip(terms, sizes)
            ]
            got = [exchange([c[q] for c in cut], stage, q) for q in range(1, count)]
            terms = [[c[0]] + [g[part] for g in got] for part, c in enumerate(cut)]
        else:
            whole = [add_up(t) for t in terms]
            got = [exchange(whole, stage, q) for q in range(1, count)]
            terms = [[v] + [g[part] for g in got] for part, v in enumerate(whole)]
    kept = [add_up(t) for t in terms]
    for number in range(halvings - 1, 0, -1):
        stage = stages[number]
        got = [exchange(kept, stage, q) for q in range(1, 1 << len(stage[0][1]))]
        kept = [
            jnp.concatenate([v] + [g[part] for g in got], axis=0)
            for part, v in enumerate(kept)
        ]
    return kept, [send(v, order[0][0], order[0][1][0]) for v, order in zip(kept, orders)]


def gram_kernel(chunks, dev_ref, row_ref, keys_ref, s_hbm, *refs):
    outs, work, s_ref, sems = refs[:4], refs[4:6], refs[6], refs[7]
    tiles = s_ref.shape[1] // TILE
    spots = places(tiles)
    piece = s_ref.shape[0] // LOADS
    copies = []
    for q in range(LOADS):
        at = pl.ds(q * piece, piece)
        copies.append(pltpu.make_async_copy(s_hbm.at[at, :], s_ref.at[at, :], sems.at[q]))
        copies[-1].start()
    for q in range(LOADS):
        copies[q].wait()
        rows = slice(q * piece, (q + 1) * piece)
        for part in range(2):
            where = {(i, j): row for i, j, row in spots[part][0]}
            for band in bands_of(tiles)[part]:
                first = band * BAND * TILE
                strip = dot(s_ref[rows, first:first + BAND * TILE], s_ref[rows, first:], 0, 0)
                for a in range(BAND):
                    i = band * BAND + a
                    for j in range(i, tiles):
                        col = (j - band * BAND) * TILE
                        row = where[(i, j)]
                        term = strip[a * TILE:(a + 1) * TILE, col:col + TILE]
                        if q:
                            term = work[part][row:row + TILE, :] + term
                        work[part][row:row + TILE, :] = term
    base = spots[0][1]
    pivots = dev_ref.shape[0]
    sub = iota((16, s_ref.shape[1]), 0)

    def pick(p, carry):
        at = row_ref[p]
        group = pl.multiple_of((at // 16) * 16, 16)
        rows = s_ref[pl.ds(group, 16), :].astype(F32)
        wanted = jnp.where(dev_ref[p] == keys_ref[2], at - group, -1)
        row = jnp.sum(jnp.where(sub == wanted, rows, 0.0), axis=0, keepdims=True)
        for t in range(tiles):
            work[0][pl.ds(base + t * pivots + p, 1), :] = row[:, t * TILE:(t + 1) * TILE]
        return carry

    lax.fori_loop(0, pivots, pick, 0, unroll=4)
    for part in range(2):
        size = work[part].shape[0] // chunks
        for q in range(chunks):
            out = outs[2 * part + q // (chunks // 2)]
            to = (q % (chunks // 2)) * size
            at = pl.multiple_of((keys_ref[part] ^ q) * size, 8)
            out[to:to + size, :] = work[part][pl.ds(at, size), :]


def local_gram(snapshots, pivot_dev, pivot_row, keys, rows, chunks):
    shapes = [jax.ShapeDtypeStruct((r // 2, TILE), F32) for r in rows for _ in range(2)]
    return pl.pallas_call(
        functools.partial(gram_kernel, chunks),
        out_shape=shapes,
        in_specs=[SMEM, SMEM, SMEM, HBM],
        out_specs=[VMEM] * 4,
        scratch_shapes=[pltpu.VMEM((r, TILE), F32) for r in rows] + [
            pltpu.VMEM(snapshots.shape, BF16),
            pltpu.SemaphoreType.DMA((LOADS,)),
        ],
        compiler_params=pltpu.CompilerParams(vmem_limit_bytes=GRANT),
        name="local_gram",
    )(in_hbm(pivot_dev), in_hbm(pivot_row), keys, in_hbm(snapshots))


def eliminate(rows, at):
    shape = rows[0].shape
    sub = iota(shape, 0)
    one = jnp.where(sub >= 0, 1.0, 0.0)

    def lane(value, j):
        return jnp.broadcast_to(value[:, j:j + 1], shape)

    def subl(value, i):
        return jnp.broadcast_to(value[i:i + 1, :], shape)

    rows = list(rows)
    count = len(rows)
    for g in range(count):
        here = rows[g]
        e = [subl(here, i) for i in range(8)]
        cols = [lane(here, at + 8 * g + j) * one for j in range(8)]
        p = [[subl(cols[j], i) if j >= i else None for j in range(8)] for i in range(8)]
        c = {h: [lane(rows[h], at + 8 * g + j) for j in range(8)] for h in range(g + 1, count)}
        scale = [None] * 8
        u = [[None] * 8 for _ in range(8)]
        for j in range(0, 8, 2):
            k = j + 1
            a, b, d = p[j][j], p[j][k], p[k][k]
            idet = 1.0 / (a * d - b * b)
            ia = 1.0 / a
            scale[j], scale[k] = ia, a * idet
            u[j][k] = b * ia
            e[k] = e[k] - u[j][k] * e[j]
            y0, y1, x0 = {}, {}, {}
            for i in range(j + 2, 8):
                y0[i] = d * p[j][i] - b * p[k][i]
                y1[i] = a * p[k][i] - b * p[j][i]
                u[j][i] = p[j][i] * ia
                u[k][i] = y1[i] * idet
                x0[i] = y0[i] * idet
            for i in range(j + 2, 8):
                for m in range(i, 8):
                    if m <= j + 3:
                        p[i][m] = p[i][m] - (y0[i] * p[j][m] + y1[i] * p[k][m]) * idet
                    else:
                        p[i][m] = p[i][m] - x0[i] * p[j][m] - u[k][i] * p[k][m]
                e[i] = e[i] - u[j][i] * e[j] - u[k][i] * e[k]
            if g + 1 < count:
                near = c[g + 1]
                z0 = (d * near[j] - b * near[k]) * idet
                z1 = (a * near[k] - b * near[j]) * idet
                rows[g + 1] = rows[g + 1] - (near[j] * ia) * e[j] - z1 * e[k]
                for m in range(j + 2, 8):
                    near[m] = near[m] - z0 * p[j][m] - z1 * p[k][m]
        if g + 2 < count:
            t = [e[i] * scale[i] for i in range(8)]
            for i in range(7, 0, -1):
                for m in range(i):
                    t[m] = t[m] - u[m][i] * t[i]
            for h in range(g + 2, count):
                rows[h] = rows[h] - add_up([c[h][j] * t[j] for j in range(8)])
        out, factor = e[0], scale[0]
        for i in range(1, 8):
            out = jnp.where(sub == i, e[i], out)
            factor = jnp.where(sub == i, scale[i], factor)
        rows[g] = out * jnp.sqrt(factor)
    return rows


def lower(value):
    return jnp.where(iota(value.shape, 1) <= iota(value.shape, 0), value, 0.0)


def product3(a, b, ca, cb):
    return dot(a[0], b[0], ca, cb) + (dot(a[0], b[1], ca, cb) + dot(a[1], b[0], ca, cb))


def twice(value):
    return tuple(jnp.concatenate([v, v], axis=0) for v in split(value))


def invert_factor(m_ref, beside=None):
    n, b = m_ref.shape[0], BLOCK
    lanes, subs = iota((b, n), 1), iota((b, n), 0)
    near, down = iota((b, TILE), 1), iota((b, TILE), 0)
    block = m_ref[:b, :TILE]
    for k in range(n // b):
        first = k * b
        tile = first // TILE * TILE
        at = first - tile
        other = b - at
        inside = (near >= at) & (near < at + b)
        eye = jnp.where(near - other == down, 1.0, 0.0)
        block = jnp.where(inside, block, eye)
        if beside is not None:
            beside(k)
        done = jnp.concatenate(
            eliminate([block[8 * g:8 * g + 8] for g in range(b // 8)], at), axis=0
        )
        inverse = split(jnp.where((near >= other) & (near - other <= down), done, 0.0))
        mine = (lanes >= first) & (lanes < first + b)
        right = m_ref[first:first + b, :]
        q = first + b
        if q < n:
            to = q // TILE * TILE
            across = product3(inverse, twice(right[:, to:to + TILE]), 1, 0)
            below = split(pltpu.roll(m_ref[q:q + b, tile:tile + TILE], b, 1))
            below = product3(below, inverse, 1, 1)
            block = m_ref[q:q + b, to:to + TILE] - product3(split(below), split(across), 1, 0)
        unit = jnp.where(lanes - first == subs, 1.0, 0.0)
        row = product3(inverse, twice(jnp.where(mine, unit, right)), 1, 0)
        m_ref[first:first + b, :] = row
        if q < n:
            high, low = split(row)
            update = dot(
                jnp.concatenate([high, high, low], axis=0),
                jnp.concatenate([high, low, high], axis=0), 0, 0)
            for r in range(q, n, b):
                m_ref[r:r + b, :] = (
                    jnp.where(mine, 0.0, m_ref[r:r + b, :]) - update[r:r + b, :]
                )


def scale_to_unit(matrix, m_ref, across_ref):
    n = matrix.shape[0]
    diagonal = jnp.where(iota((n, n), 0) == iota((n, n), 1), matrix, 0.0)
    down = lax.rsqrt(jnp.sum(diagonal, axis=1, keepdims=True))
    across = lax.rsqrt(jnp.sum(diagonal, axis=0, keepdims=True))
    m_ref[...] = matrix * down * across
    across_ref[...] = across


def solve_kernel(
    chunks, rows_total, keys_ref, start_ref, s_ref, a0_ref, a1_ref, b0_ref, b1_ref,
    modes_hbm, scores_ref, basis_ref, pa_ref, pb_ref, gh_ref, gl_ref, xh_ref, xl_ref,
    yh_ref, yl_ref, z_ref, m_ref, across_ref, factor_ref, rows_ref, high_ref, sem,
):
    packed = (pa_ref, pb_ref)
    halves = ((a0_ref, a1_ref), (b0_ref, b1_ref))
    snap, rank = start_ref.shape
    tiles = snap // TILE
    for part in range(2):
        size = packed[part].shape[0] // chunks
        for q in range(chunks):
            half = halves[part][q // (chunks // 2)]
            at = (q % (chunks // 2)) * size
            to = pl.multiple_of((keys_ref[part] ^ q) * size, 8)
            packed[part][pl.ds(to, size), :] = half[at:at + size, :]
    spots = places(tiles)
    for part in range(2):
        for i, j, row in spots[part][0]:
            value = packed[part][row:row + TILE, :]
            high, low = split(value)
            gh_ref[i * TILE:(i + 1) * TILE, j * TILE:(j + 1) * TILE] = high
            gl_ref[i * TILE:(i + 1) * TILE, j * TILE:(j + 1) * TILE] = low
            if i != j:
                high, low = split(jnp.transpose(value))
                gh_ref[j * TILE:(j + 1) * TILE, i * TILE:(i + 1) * TILE] = high
                gl_ref[j * TILE:(j + 1) * TILE, i * TILE:(i + 1) * TILE] = low
    strips = rank // BLOCK
    step = snap // strips

    def product(at, xh, xl):
        gh = gh_ref[at, :]
        return dot(gh, xh, 1, 0) + (dot(gh, xl, 1, 0) + dot(gl_ref[at, :], xh, 1, 0))

    yh_ref[...], yl_ref[...] = split(start_ref[...])
    for r in range(strips):
        at = pl.ds(r * step, step)
        z_ref[at, :] = product(at, yh_ref[...], yl_ref[...])
    square = 0.0
    for r in range(strips):
        at = pl.ds(r * step, step)
        yh, yl = split(z_ref[at, :])
        yh_ref[at, :], yl_ref[at, :] = yh, yl
        square = square + dot(yh, yh, 0, 0)
    scale_to_unit(square, m_ref, across_ref)

    def iteration(number, carry):
        def beside(k):
            at = pl.ds(k * step, step)
            z_ref[at, :] = product(at, yh_ref[...], yl_ref[...])

        invert_factor(m_ref, beside)
        factor_ref[...] = (lower(m_ref[...]) * across_ref[...]).astype(BF16)

        @pl.when(number == ITERS - 1)
        def _():
            factor = factor_ref[...]
            iterate = dot(yh_ref[...], factor, 1, 1) + dot(yl_ref[...], factor, 1, 1)
            xh_ref[...], xl_ref[...] = split(iterate)

        factor = factor_ref[...]
        square = 0.0
        for r in range(strips):
            at = pl.ds(r * step, step)
            zh, zl = split(z_ref[at, :])
            yh, yl = split(dot(zh, factor, 1, 1) + dot(zl, factor, 1, 1))
            yh_ref[at, :], yl_ref[at, :] = yh, yl
            square = square + dot(yh, yh, 0, 0)
        scale_to_unit(square, m_ref, across_ref)
        return carry

    lax.fori_loop(0, ITERS, iteration, 0)
    yh, yl = yh_ref[...], yl_ref[...]
    xh, xl = xh_ref[...], xl_ref[...]
    small = dot(xh, yh, 0, 0) + (dot(xh, yl, 0, 0) + dot(xl, yh, 0, 0))
    scale_to_unit((small + jnp.transpose(small)) * (0.5 / rows_total), m_ref, across_ref)
    invert_factor(m_ref)
    fh, fl = split(lower(m_ref[...]) * across_ref[...])
    coef = (dot(xh, fh, 1, 1) + (dot(xh, fl, 1, 1) + dot(xl, fh, 1, 1))).astype(BF16)
    chunk = 512
    spans = [pl.ds(r * chunk, chunk) for r in range(s_ref.shape[0] // chunk)]
    for at in spans:
        basis = dot(s_ref[at, :], coef, 1, 0)
        rows_ref[at, :] = basis
        high_ref[at, :] = basis.astype(BF16)
    base = spots[0][1]
    pivots = basis_ref.shape[0]
    picked = jnp.concatenate(
        [pa_ref[base + t * pivots:base + (t + 1) * pivots, :] for t in range(tiles)], axis=1
    )
    panel = dot(picked.astype(BF16), coef, 1, 0)
    gram = dot(panel, panel, 1, 1, HIGHEST)
    same = iota((pivots, pivots), 0) == iota((pivots, pivots), 1)
    diagonal = jnp.where(same, gram, 0.0)
    down = lax.rsqrt(jnp.sum(diagonal, axis=1, keepdims=True))
    across = lax.rsqrt(jnp.sum(diagonal, axis=0, keepdims=True))
    wide = jnp.concatenate(
        [gram * down * across, jnp.where(same, 1.0, 0.0)]
        + [jnp.zeros((pivots, TILE - 2 * pivots), F32)], axis=1
    )
    done = eliminate([wide[8 * g:8 * g + 8] for g in range(pivots // 8)], 0)
    factor = lower(jnp.concatenate(done, axis=0)[:, pivots:2 * pivots]) * across
    turned = dot(factor, panel, 1, 0, HIGHEST)
    basis_ref[...] = turned
    th, tl = split(turned)
    thrice_h = jnp.concatenate([th, th, th], axis=0)
    thrice_l = jnp.concatenate([tl, tl, tl], axis=0)
    stacked = jnp.concatenate([th, tl, th], axis=0)
    from_low = iota((chunk, 3 * pivots), 1) >= 2 * pivots
    ones = jnp.ones((8, rank), BF16)
    store = pltpu.make_async_copy(high_ref, modes_hbm, sem)
    store.start()

    def project(r, carry):
        at = pl.ds(pl.multiple_of(r * chunk, chunk), chunk)
        basis, high = rows_ref[at, :], high_ref[at, :]
        coeffs = dot(high, thrice_h, 1, 1) + dot(high, thrice_l, 1, 1)
        ch, cl = split(coeffs)
        left = basis - dot(jnp.where(from_low, cl, ch), stacked, 1, 0)
        qh, ql = split(left * left)
        total = (dot(ones, qh, 1, 1) + dot(ones, ql, 1, 1)) * (1.0 / rank)
        scores_ref[:, at] = total[0:1, :]
        return carry

    lax.fori_loop(0, len(spans), project, 0, unroll=2)
    store.wait()


def solve(snapshots, start, keys, pieces, pivots, rows, chunks, rows_total):
    snap, rank = start.shape
    here = snapshots.shape[0]
    return pl.pallas_call(
        functools.partial(solve_kernel, chunks, rows_total),
        out_shape=[
            jax.ShapeDtypeStruct((here, rank), BF16),
            jax.ShapeDtypeStruct((1, here), F32),
            jax.ShapeDtypeStruct((pivots, rank), F32),
        ],
        in_specs=[SMEM] + [VMEM] * 6,
        out_specs=[HBM, VMEM, VMEM],
        scratch_shapes=[pltpu.VMEM((r, TILE), F32) for r in rows] + [
            pltpu.VMEM((snap, snap), BF16),
            pltpu.VMEM((snap, snap), BF16),
            pltpu.VMEM((snap, rank), BF16),
            pltpu.VMEM((snap, rank), BF16),
            pltpu.VMEM((snap, rank), BF16),
            pltpu.VMEM((snap, rank), BF16),
            pltpu.VMEM((snap, rank), F32),
            pltpu.VMEM((rank, rank), F32),
            pltpu.VMEM((1, rank), F32),
            pltpu.VMEM((rank, rank), BF16),
            pltpu.VMEM((here, rank), F32),
            pltpu.VMEM((here, rank), BF16),
            pltpu.SemaphoreType.DMA,
        ],
        compiler_params=pltpu.CompilerParams(vmem_limit_bytes=GRANT),
        name="solve",
    )(keys, start, snapshots, *pieces)


def local(mesh_shape, snapshots, start, pivot_dev, pivot_row):
    here, snap = snapshots.shape
    pivots = pivot_dev.shape[0]
    spots = places(snap // TILE)
    rows = [spots[0][1] + pivots * (snap // TILE), spots[1][1]]
    orders, halvings = exchange_plan(mesh_shape, rows)
    chunks = chunks_of(orders[0], halvings)
    myself = lax.axis_index(("grp", "blk"))
    keys = jnp.stack([key_of(orders[0], halvings), key_of(orders[1], halvings), myself])
    a0, a1, b0, b1 = local_gram(snapshots, pivot_dev, pivot_row, keys, rows, chunks)
    own, other = reduce_parts([a0, b0], [a1, b1], orders, halvings)
    pieces = (own[0], other[0], own[1], other[1])
    rows_total = here * mesh_shape["grp"] * mesh_shape["blk"]
    modes, scores, basis = solve(
        snapshots, start, keys, pieces, pivots, rows, chunks, rows_total
    )
    return modes, scores.reshape(here), basis.T


def solution(mesh):
    placed = (P(("grp", "blk"), None), P(), P(), P())
    return jax.shard_map(
        functools.partial(local, dict(mesh.shape)),
        mesh=mesh,
        in_specs=placed,
        out_specs=(P(("grp", "blk"), None), P(("grp", "blk")), P()),
        check_vma=False,
    )
```

```python
import functools
import jax
import jax.numpy as jnp
from jax import lax
from jax.experimental import pallas as pl
from jax.experimental.pallas import tpu as pltpu
from jax.sharding import PartitionSpec as P


ITERS = 4
TILE = 128
BAND = 2
BLOCK = 64
LOADS = 2
UNIT = 256
GRANT = 28 << 20
F32, BF16 = jnp.float32, jnp.bfloat16
HIGHEST = lax.Precision.HIGHEST
VMEM = pl.BlockSpec(memory_space=pltpu.VMEM)
SMEM = pl.BlockSpec(memory_space=pltpu.SMEM)
HBM = pl.BlockSpec(memory_space=pltpu.HBM)


def dot(a, b, ca, cb, precision=None):
    return lax.dot_general(
        a, b, (((ca,), (cb,)), ((), ())), precision=precision, preferred_element_type=F32
    )


def split(value):
    high = value.astype(BF16)
    return high, (value - high.astype(F32)).astype(BF16)


def in_hbm(value):
    return pltpu.with_memory_space_constraint(value, pltpu.HBM)


def iota(shape, dim):
    return lax.broadcasted_iota(jnp.int32, shape, dim)


def bands_of(tiles):
    count = tiles // BAND
    outer = [0, count - 1] if count > 1 else [0]
    return outer, [band for band in range(count) if band not in outer]


def places(tiles):
    result = []
    for bands in bands_of(tiles):
        row, above, pairs = 0, [], []
        for band in bands:
            for i in range(band * BAND, band * BAND + BAND):
                for j in range(i + 1, tiles):
                    above.append((i, j, row))
                    row += TILE
            pairs.append((band, row))
            row += TILE
        result.append((above, pairs, row))
    return result


def part_rows(tiles, pivots):
    first, second = places(tiles)
    ends = (first[2] + pivots * tiles, second[2] + tiles // BAND)
    return [-(-end // UNIT) * UNIT for end in ends]


def exchange_plan(mesh_shape, rows):
    grp = [("grp", (1 << b,)) for b in range(mesh_shape["grp"].bit_length() - 1)]
    blk = [("blk", (1 << b,)) for b in range(mesh_shape["blk"].bit_length() - 1)]
    pair = [("blk", blk[1][1] + blk[2][1])] if len(blk) > 2 else blk[1:2]
    rest = pair + blk[3:] + grp[2:]
    orders = (grp[:1] + blk[:1] + grp[1:2] + rest, grp[:1] + grp[1:2] + blk[:1] + rest)
    halvings, ways = 0, 1
    for _, masks in orders[0]:
        ways *= 1 << len(masks)
        if any(r % (8 * ways) for r in rows):
            break
        halvings += 1
    return orders, halvings


def chunks_of(order, halvings):
    return 1 << sum(len(masks) for _, masks in order[:halvings])


def key_of(order, halvings):
    key = jnp.int32(0)
    for axis, masks in order[:halvings]:
        for mask in masks:
            key = key * 2 + jnp.where((lax.axis_index(axis) & mask) != 0, 1, 0)
    return key


def partners(masks):
    result = [0]
    for mask in masks:
        result = [m ^ extra for m in result for extra in (0, mask)]
    return result


def send(value, axis, mask):
    size = lax.axis_size(axis)
    return lax.ppermute(value, axis, [(i, i ^ mask) for i in range(size)])


def exchange(values, stages, mask_at):
    if all(stage == stages[0] for stage in stages):
        axis, masks = stages[0]
        got = send(jnp.concatenate(values, axis=0), axis, partners(masks)[mask_at])
        first = values[0].shape[0]
        return [got[:first], got[first:]]
    result = []
    for value, (axis, masks) in zip(values, stages):
        result.append(send(value, axis, partners(masks)[mask_at]))
    return result


def add_up(terms):
    while len(terms) > 1:
        terms = [a + b for a, b in zip(terms[::2], terms[1::2])]
    return terms[0]


def reduce_parts(kept, sent, orders, halvings):
    stages = list(zip(*orders))
    terms = []
    for v, s, order in zip(kept, sent, orders):
        terms.append([v, send(s, order[0][0], order[0][1][0])])
    for number in range(1, len(stages)):
        stage = stages[number]
        count = 1 << len(stage[0][1])
        if number < halvings:
            sizes = [t[0].shape[0] // count for t in terms]
            cut = [
                [add_up([v[q * size:(q + 1) * size] for v in t]) for q in range(count)]
                for t, size in zip(terms, sizes)
            ]
            got = []
            for q in range(1, count):
                got.append(exchange([c[q] for c in cut], stage, q))
            terms = [[c[0]] + [g[part] for g in got] for part, c in enumerate(cut)]
        else:
            whole = [add_up(t) for t in terms]
            got = [exchange(whole, stage, q) for q in range(1, count)]
            terms = [[v] + [g[part] for g in got] for part, v in enumerate(whole)]
    kept = [add_up(t) for t in terms]
    for number in range(halvings - 1, 0, -1):
        stage = stages[number]
        got = [exchange(kept, stage, q) for q in range(1, 1 << len(stage[0][1]))]
        kept = [
            jnp.concatenate([v] + [g[part] for g in got], axis=0)
            for part, v in enumerate(kept)
        ]
    return kept, [send(v, order[0][0], order[0][1][0]) for v, order in zip(kept, orders)]


def gram_kernel(chunks, dev_ref, row_ref, keys_ref, s_hbm, *refs):
    outs, work, s_ref, sems = refs[:4], refs[4:6], refs[6], refs[7]
    tiles = s_ref.shape[1] // TILE
    spots = places(tiles)
    piece = s_ref.shape[0] // LOADS
    upper = iota((TILE, TILE), 0) <= iota((TILE, TILE), 1)
    same = iota((TILE, TILE), 0) == iota((TILE, TILE), 1)
    last = spots[1][2]
    work[1][last:, :] = jnp.zeros_like(work[1][last:, :])
    copies = []
    for q in range(LOADS):
        at = pl.ds(q * piece, piece)
        copies.append(pltpu.make_async_copy(s_hbm.at[at, :], s_ref.at[at, :], sems.at[q]))
        copies[-1].start()
    for q in range(LOADS):
        copies[q].wait()
        rows = slice(q * piece, (q + 1) * piece)
        for part in range(2):
            above, pairs, _ = spots[part]
            where = {(i, j): row for i, j, row in above}
            for band, pair_row in pairs:
                first = band * BAND * TILE
                strip = dot(s_ref[rows, first:first + BAND * TILE], s_ref[rows, first:], 0, 0)

                def tile(a, b):
                    return strip[a * TILE:(a + 1) * TILE, b * TILE:(b + 1) * TILE]

                terms = [
                    (part, where[(i, j)], tile(i - band * BAND, j - band * BAND))
                    for i in range(band * BAND, band * BAND + BAND) for j in range(i + 1, tiles)
                ]
                terms.append((part, pair_row, jnp.where(upper, tile(0, 0), tile(1, 1))))
                diagonal = jnp.sum(jnp.where(same, tile(1, 1), 0.0), axis=0, keepdims=True)
                terms.append((1, spots[1][2] + band, diagonal))
                for to, row, term in terms:
                    size = term.shape[0]
                    if q:
                        term = work[to][row:row + size, :] + term
                    work[to][row:row + size, :] = term
    base = spots[0][2]
    pivots = dev_ref.shape[0]
    sub = iota((16, s_ref.shape[1]), 0)

    def pick(p, carry):
        at = row_ref[p]
        group = pl.multiple_of((at // 16) * 16, 16)
        rows = s_ref[pl.ds(group, 16), :].astype(F32)
        wanted = jnp.where(dev_ref[p] == keys_ref[2], at - group, -1)
        row = jnp.sum(jnp.where(sub == wanted, rows, 0.0), axis=0, keepdims=True)
        for t in range(tiles):
            work[0][pl.ds(base + t * pivots + p, 1), :] = row[:, t * TILE:(t + 1) * TILE]
        return carry

    lax.fori_loop(0, pivots, pick, 0, unroll=4)
    for part in range(2):
        size = work[part].shape[0] // chunks
        for q in range(chunks):
            out = outs[2 * part + q // (chunks // 2)]
            to = (q % (chunks // 2)) * size
            at = pl.multiple_of((keys_ref[part] ^ q) * size, 8)
            out[to:to + size, :] = work[part][pl.ds(at, size), :]


def local_gram(snapshots, pivot_dev, pivot_row, keys, rows, chunks):
    shapes = [jax.ShapeDtypeStruct((r // 2, TILE), F32) for r in rows for _ in range(2)]
    return pl.pallas_call(
        functools.partial(gram_kernel, chunks),
        out_shape=shapes,
        in_specs=[SMEM, SMEM, SMEM, HBM],
        out_specs=[VMEM] * 4,
        scratch_shapes=[pltpu.VMEM((r, TILE), F32) for r in rows] + [
            pltpu.VMEM(snapshots.shape, BF16),
            pltpu.SemaphoreType.DMA((LOADS,)),
        ],
        compiler_params=pltpu.CompilerParams(vmem_limit_bytes=GRANT),
        name="local_gram",
    )(in_hbm(pivot_dev), in_hbm(pivot_row), keys, in_hbm(snapshots))


def eliminate(rows, at):
    shape = rows[0].shape
    sub = iota(shape, 0)
    one = jnp.where(sub >= 0, 1.0, 0.0)

    def lane(value, j):
        return jnp.broadcast_to(value[:, j:j + 1], shape)

    def subl(value, i):
        return jnp.broadcast_to(value[i:i + 1, :], shape)

    rows = list(rows)
    count = len(rows)
    for g in range(count):
        here = rows[g]
        e = [subl(here, i) for i in range(8)]
        cols = [lane(here, at + 8 * g + j) * one for j in range(8)]
        p = [[subl(cols[j], i) if j >= i else None for j in range(8)] for i in range(8)]
        c = {h: [lane(rows[h], at + 8 * g + j) for j in range(8)] for h in range(g + 1, count)}
        scale = [None] * 8
        u = [[None] * 8 for _ in range(8)]
        for j in range(0, 8, 2):
            k = j + 1
            a, b, d = p[j][j], p[j][k], p[k][k]
            idet = 1.0 / (a * d - b * b)
            ia = 1.0 / a
            scale[j], scale[k] = ia, a * idet
            u[j][k] = b * ia
            e[k] = e[k] - u[j][k] * e[j]
            y0, y1, x0 = {}, {}, {}
            for i in range(j + 2, 8):
                y0[i] = d * p[j][i] - b * p[k][i]
                y1[i] = a * p[k][i] - b * p[j][i]
                u[j][i] = p[j][i] * ia
                u[k][i] = y1[i] * idet
                x0[i] = y0[i] * idet
            for i in range(j + 2, 8):
                for m in range(i, 8):
                    if m <= j + 3:
                        p[i][m] = p[i][m] - (y0[i] * p[j][m] + y1[i] * p[k][m]) * idet
                    else:
                        p[i][m] = p[i][m] - x0[i] * p[j][m] - u[k][i] * p[k][m]
                e[i] = e[i] - u[j][i] * e[j] - u[k][i] * e[k]
            if g + 1 < count:
                near = c[g + 1]
                z0 = (d * near[j] - b * near[k]) * idet
                z1 = (a * near[k] - b * near[j]) * idet
                rows[g + 1] = rows[g + 1] - (near[j] * ia) * e[j] - z1 * e[k]
                for m in range(j + 2, 8):
                    near[m] = near[m] - z0 * p[j][m] - z1 * p[k][m]
        if g + 2 < count:
            t = [e[i] * scale[i] for i in range(8)]
            for i in range(7, 0, -1):
                for m in range(i):
                    t[m] = t[m] - u[m][i] * t[i]
            for h in range(g + 2, count):
                rows[h] = rows[h] - add_up([c[h][j] * t[j] for j in range(8)])
        out, factor = e[0], scale[0]
        for i in range(1, 8):
            out = jnp.where(sub == i, e[i], out)
            factor = jnp.where(sub == i, scale[i], factor)
        rows[g] = out * jnp.sqrt(factor)
    return rows


def lower(value):
    return jnp.where(iota(value.shape, 1) <= iota(value.shape, 0), value, 0.0)


def product3(a, b, ca, cb):
    return dot(a[0], b[0], ca, cb) + (dot(a[0], b[1], ca, cb) + dot(a[1], b[0], ca, cb))


def twice(value):
    return tuple(jnp.concatenate([v, v], axis=0) for v in split(value))


def invert_factor(m_ref, beside=None):
    n, b = m_ref.shape[0], BLOCK
    lanes, subs = iota((b, n), 1), iota((b, n), 0)
    near, down = iota((b, TILE), 1), iota((b, TILE), 0)
    block = m_ref[:b, :TILE]
    for k in range(n // b):
        first = k * b
        tile = first // TILE * TILE
        at = first - tile
        other = b - at
        inside = (near >= at) & (near < at + b)
        eye = jnp.where(near - other == down, 1.0, 0.0)
        block = jnp.where(inside, block, eye)
        if beside is not None:
            beside(k)
        done = jnp.concatenate(
            eliminate([block[8 * g:8 * g + 8] for g in range(b // 8)], at), axis=0
        )
        inverse = split(jnp.where((near >= other) & (near - other <= down), done, 0.0))
        mine = (lanes >= first) & (lanes < first + b)
        right = m_ref[first:first + b, :]
        q = first + b
        if q < n:
            to = q // TILE * TILE
            across = product3(inverse, twice(right[:, to:to + TILE]), 1, 0)
            below = split(pltpu.roll(m_ref[q:q + b, tile:tile + TILE], b, 1))
            below = product3(below, inverse, 1, 1)
            block = m_ref[q:q + b, to:to + TILE] - product3(split(below), split(across), 1, 0)
        unit = jnp.where(lanes - first == subs, 1.0, 0.0)
        row = product3(inverse, twice(jnp.where(mine, unit, right)), 1, 0)
        m_ref[first:first + b, :] = row
        if q < n:
            high, low = split(row)
            update = dot(
                jnp.concatenate([high, high, low], axis=0),
                jnp.concatenate([high, low, high], axis=0), 0, 0)
            for r in range(q, n, b):
                m_ref[r:r + b, :] = (
                    jnp.where(mine, 0.0, m_ref[r:r + b, :]) - update[r:r + b, :]
                )


def scale_to_unit(matrix, m_ref, across_ref):
    n = matrix.shape[0]
    diagonal = jnp.where(iota((n, n), 0) == iota((n, n), 1), matrix, 0.0)
    down = lax.rsqrt(jnp.sum(diagonal, axis=1, keepdims=True))
    across = lax.rsqrt(jnp.sum(diagonal, axis=0, keepdims=True))
    m_ref[...] = matrix * down * across
    across_ref[...] = across


def solve_kernel(
    chunks, rows_total, keys_ref, start_ref, s_ref, a0_ref, a1_ref, b0_ref, b1_ref,
    modes_hbm, scores_ref, basis_ref, pa_ref, pb_ref, gh_ref, gl_ref, xh_ref, xl_ref,
    yh_ref, yl_ref, z_ref, m_ref, across_ref, factor_ref, rows_ref, high_ref, sem,
):
    packed = (pa_ref, pb_ref)
    halves = ((a0_ref, a1_ref), (b0_ref, b1_ref))
    snap, rank = start_ref.shape
    tiles = snap // TILE
    for part in range(2):
        size = packed[part].shape[0] // chunks
        for q in range(chunks):
            half = halves[part][q // (chunks // 2)]
            at = (q % (chunks // 2)) * size
            to = pl.multiple_of((keys_ref[part] ^ q) * size, 8)
            packed[part][pl.ds(to, size), :] = half[at:at + size, :]
    spots = places(tiles)

    def put(i, j, value):
        high, low = split(value)
        gh_ref[i * TILE:(i + 1) * TILE, j * TILE:(j + 1) * TILE] = high
        gl_ref[i * TILE:(i + 1) * TILE, j * TILE:(j + 1) * TILE] = low

    across, along = iota((TILE, TILE), 0), iota((TILE, TILE), 1)
    for part in range(2):
        for i, j, row in spots[part][0]:
            value = packed[part][row:row + TILE, :]
            put(i, j, value)
            put(j, i, jnp.transpose(value))
        for band, row in spots[part][1]:
            value = packed[part][row:row + TILE, :]
            turned = jnp.transpose(value)
            end = spots[1][2] + band
            diagonal = jnp.where(across == along, pb_ref[end:end + 1, :], turned)
            i = band * BAND
            put(i, i, jnp.where(across <= along, value, turned))
            put(i + 1, i + 1, jnp.where(across > along, value, diagonal))
    strips = rank // BLOCK
    step = snap // strips

    def product(at, xh, xl):
        gh = gh_ref[at, :]
        return dot(gh, xh, 1, 0) + (dot(gh, xl, 1, 0) + dot(gl_ref[at, :], xh, 1, 0))

    yh_ref[...], yl_ref[...] = split(start_ref[...])
    for r in range(strips):
        at = pl.ds(r * step, step)
        z_ref[at, :] = product(at, yh_ref[...], yl_ref[...])
    square = 0.0
    for r in range(strips):
        at = pl.ds(r * step, step)
        yh, yl = split(z_ref[at, :])
        yh_ref[at, :], yl_ref[at, :] = yh, yl
        square = square + dot(yh, yh, 0, 0)
    scale_to_unit(square, m_ref, across_ref)

    def iteration(number, carry):
        def beside(k):
            at = pl.ds(k * step, step)
            z_ref[at, :] = product(at, yh_ref[...], yl_ref[...])

        invert_factor(m_ref, beside)
        factor_ref[...] = (lower(m_ref[...]) * across_ref[...]).astype(BF16)

        @pl.when(number == ITERS - 1)
        def _():
            factor = factor_ref[...]
            iterate = dot(yh_ref[...], factor, 1, 1) + dot(yl_ref[...], factor, 1, 1)
            xh_ref[...], xl_ref[...] = split(iterate)

        factor = factor_ref[...]
        square = 0.0
        for r in range(strips):
            at = pl.ds(r * step, step)
            zh, zl = split(z_ref[at, :])
            yh, yl = split(dot(zh, factor, 1, 1) + dot(zl, factor, 1, 1))
            yh_ref[at, :], yl_ref[at, :] = yh, yl
            square = square + dot(yh, yh, 0, 0)
        scale_to_unit(square, m_ref, across_ref)
        return carry

    lax.fori_loop(0, ITERS, iteration, 0)
    yh, yl = yh_ref[...], yl_ref[...]
    xh, xl = xh_ref[...], xl_ref[...]
    small = dot(xh, yh, 0, 0) + (dot(xh, yl, 0, 0) + dot(xl, yh, 0, 0))
    scale_to_unit((small + jnp.transpose(small)) * (0.5 / rows_total), m_ref, across_ref)
    invert_factor(m_ref)
    fh, fl = split(lower(m_ref[...]) * across_ref[...])
    coef = (dot(xh, fh, 1, 1) + (dot(xh, fl, 1, 1) + dot(xl, fh, 1, 1))).astype(BF16)
    chunk = 512
    spans = [pl.ds(r * chunk, chunk) for r in range(s_ref.shape[0] // chunk)]
    for at in spans:
        basis = dot(s_ref[at, :], coef, 1, 0)
        rows_ref[at, :] = basis
        high_ref[at, :] = basis.astype(BF16)
    base = spots[0][2]
    pivots = basis_ref.shape[0]
    picked = jnp.concatenate(
        [pa_ref[base + t * pivots:base + (t + 1) * pivots, :] for t in range(tiles)], axis=1
    )
    panel = dot(picked.astype(BF16), coef, 1, 0)
    gram = dot(panel, panel, 1, 1, HIGHEST)
    same = iota((pivots, pivots), 0) == iota((pivots, pivots), 1)
    diagonal = jnp.where(same, gram, 0.0)
    down = lax.rsqrt(jnp.sum(diagonal, axis=1, keepdims=True))
    across = lax.rsqrt(jnp.sum(diagonal, axis=0, keepdims=True))
    wide = jnp.concatenate(
        [gram * down * across, jnp.where(same, 1.0, 0.0)]
        + [jnp.zeros((pivots, TILE - 2 * pivots), F32)], axis=1
    )
    done = eliminate([wide[8 * g:8 * g + 8] for g in range(pivots // 8)], 0)
    factor = lower(jnp.concatenate(done, axis=0)[:, pivots:2 * pivots]) * across
    turned = dot(factor, panel, 1, 0, HIGHEST)
    basis_ref[...] = turned
    th, tl = split(turned)
    thrice_h = jnp.concatenate([th, th, th], axis=0)
    thrice_l = jnp.concatenate([tl, tl, tl], axis=0)
    stacked = jnp.concatenate([th, tl, th], axis=0)
    from_low = iota((chunk, 3 * pivots), 1) >= 2 * pivots
    ones = jnp.ones((8, rank), BF16)
    store = pltpu.make_async_copy(high_ref, modes_hbm, sem)
    store.start()

    def project(r, carry):
        at = pl.ds(pl.multiple_of(r * chunk, chunk), chunk)
        basis, high = rows_ref[at, :], high_ref[at, :]
        coeffs = dot(high, thrice_h, 1, 1) + dot(high, thrice_l, 1, 1)
        ch, cl = split(coeffs)
        left = basis - dot(jnp.where(from_low, cl, ch), stacked, 1, 0)
        qh, ql = split(left * left)
        total = (dot(ones, qh, 1, 1) + dot(ones, ql, 1, 1)) * (1.0 / rank)
        scores_ref[:, at] = total[0:1, :]
        return carry

    lax.fori_loop(0, len(spans), project, 0, unroll=2)
    store.wait()


def solve(snapshots, start, keys, pieces, pivots, rows, chunks, rows_total):
    snap, rank = start.shape
    here = snapshots.shape[0]
    return pl.pallas_call(
        functools.partial(solve_kernel, chunks, rows_total),
        out_shape=[
            jax.ShapeDtypeStruct((here, rank), BF16),
            jax.ShapeDtypeStruct((1, here), F32),
            jax.ShapeDtypeStruct((pivots, rank), F32),
        ],
        in_specs=[SMEM] + [VMEM] * 6,
        out_specs=[HBM, VMEM, VMEM],
        scratch_shapes=[pltpu.VMEM((r, TILE), F32) for r in rows] + [
            pltpu.VMEM((snap, snap), BF16),
            pltpu.VMEM((snap, snap), BF16),
            pltpu.VMEM((snap, rank), BF16),
            pltpu.VMEM((snap, rank), BF16),
            pltpu.VMEM((snap, rank), BF16),
            pltpu.VMEM((snap, rank), BF16),
            pltpu.VMEM((snap, rank), F32),
            pltpu.VMEM((rank, rank), F32),
            pltpu.VMEM((1, rank), F32),
            pltpu.VMEM((rank, rank), BF16),
            pltpu.VMEM((here, rank), F32),
            pltpu.VMEM((here, rank), BF16),
            pltpu.SemaphoreType.DMA,
        ],
        compiler_params=pltpu.CompilerParams(vmem_limit_bytes=GRANT),
        name="solve",
    )(keys, start, snapshots, *pieces)


def local(mesh_shape, snapshots, start, pivot_dev, pivot_row):
    here, snap = snapshots.shape
    pivots = pivot_dev.shape[0]
    rows = part_rows(snap // TILE, pivots)
    orders, halvings = exchange_plan(mesh_shape, rows)
    chunks = chunks_of(orders[0], halvings)
    myself = lax.axis_index(("grp", "blk"))
    keys = jnp.stack([key_of(orders[0], halvings), key_of(orders[1], halvings), myself])
    a0, a1, b0, b1 = local_gram(snapshots, pivot_dev, pivot_row, keys, rows, chunks)
    own, other = reduce_parts([a0, b0], [a1, b1], orders, halvings)
    pieces = (own[0], other[0], own[1], other[1])
    rows_total = here * mesh_shape["grp"] * mesh_shape["blk"]
    modes, scores, basis = solve(
        snapshots, start, keys, pieces, pivots, rows, chunks, rows_total
    )
    return modes, scores.reshape(here), basis.T


def solution(mesh):
    placed = (P(("grp", "blk"), None), P(), P(), P())

    def body(*args):
        return local(dict(mesh.shape), *args)

    return jax.shard_map(
        body,
        mesh=mesh,
        in_specs=placed,
        out_specs=(P(("grp", "blk"), None), P(("grp", "blk")), P()),
        check_vma=False,
    )
```

```python
import functools
import jax
import jax.numpy as jnp
from jax import lax
from jax.experimental import pallas as pl
from jax.experimental.pallas import tpu as pltpu
from jax.sharding import PartitionSpec as P


ITERS = 4
TILE = 128
BAND = 2
BLOCK = 64
LOADS = 2
UNIT = 256
GRANT = 28 << 20
F32, BF16 = jnp.float32, jnp.bfloat16
HIGHEST = lax.Precision.HIGHEST
VMEM = pl.BlockSpec(memory_space=pltpu.VMEM)
SMEM = pl.BlockSpec(memory_space=pltpu.SMEM)
HBM = pl.BlockSpec(memory_space=pltpu.HBM)


def dot(a, b, ca, cb, precision=None):
    return lax.dot_general(
        a, b, (((ca,), (cb,)), ((), ())), precision=precision, preferred_element_type=F32
    )


def split(value):
    high = value.astype(BF16)
    return high, (value - high.astype(F32)).astype(BF16)


def in_hbm(value):
    return pltpu.with_memory_space_constraint(value, pltpu.HBM)


def iota(shape, dim):
    return lax.broadcasted_iota(jnp.int32, shape, dim)


def bands_of(tiles):
    count = tiles // BAND
    outer = [0, count - 1] if count > 1 else [0]
    return outer, [band for band in range(count) if band not in outer]


def places(tiles):
    result = []
    for bands in bands_of(tiles):
        row, above, pairs = 0, [], []
        for band in bands:
            for i in range(band * BAND, band * BAND + BAND):
                for j in range(i + 1, tiles):
                    above.append((i, j, row))
                    row += TILE
            pairs.append((band, row))
            row += TILE
        result.append((above, pairs, row))
    return result


def part_rows(tiles, pivots):
    first, second = places(tiles)
    ends = (first[2] + pivots * tiles, second[2] + tiles // BAND)
    return [-(-end // UNIT) * UNIT for end in ends]


def exchange_plan(mesh_shape, rows):
    grp = [("grp", (1 << b,)) for b in range(mesh_shape["grp"].bit_length() - 1)]
    blk = [("blk", (1 << b,)) for b in range(mesh_shape["blk"].bit_length() - 1)]
    pair = [("blk", blk[1][1] + blk[2][1])] if len(blk) > 2 else blk[1:2]
    rest = pair + blk[3:] + grp[2:]
    orders = (grp[:1] + blk[:1] + grp[1:2] + rest, grp[:1] + grp[1:2] + blk[:1] + rest)
    halvings, ways = 0, 1
    for _, masks in orders[0]:
        ways *= 1 << len(masks)
        if any(r % (8 * ways) for r in rows):
            break
        halvings += 1
    return orders, halvings


def chunks_of(order, halvings):
    return 1 << sum(len(masks) for _, masks in order[:halvings])


def key_of(order, halvings):
    key = jnp.int32(0)
    for axis, masks in order[:halvings]:
        for mask in masks:
            key = key * 2 + jnp.where((lax.axis_index(axis) & mask) != 0, 1, 0)
    return key


def partners(masks):
    result = [0]
    for mask in masks:
        result = [m ^ extra for m in result for extra in (0, mask)]
    return result


def send(value, axis, mask):
    size = lax.axis_size(axis)
    return lax.ppermute(value, axis, [(i, i ^ mask) for i in range(size)])


def exchange(values, stages, mask_at):
    if all(stage == stages[0] for stage in stages):
        axis, masks = stages[0]
        got = send(jnp.concatenate(values, axis=0), axis, partners(masks)[mask_at])
        first = values[0].shape[0]
        return [got[:first], got[first:]]
    result = []
    for value, (axis, masks) in zip(values, stages):
        result.append(send(value, axis, partners(masks)[mask_at]))
    return result


def add_up(terms):
    while len(terms) > 1:
        terms = [a + b for a, b in zip(terms[::2], terms[1::2])]
    return terms[0]


def reduce_parts(kept, sent, orders, halvings):
    stages = list(zip(*orders))
    terms = []
    for v, s, order in zip(kept, sent, orders):
        terms.append([v, send(s, order[0][0], order[0][1][0])])
    for number in range(1, len(stages)):
        stage = stages[number]
        count = 1 << len(stage[0][1])
        if number < halvings:
            sizes = [t[0].shape[0] // count for t in terms]
            cut = [
                [add_up([v[q * size:(q + 1) * size] for v in t]) for q in range(count)]
                for t, size in zip(terms, sizes)
            ]
            got = []
            for q in range(1, count):
                got.append(exchange([c[q] for c in cut], stage, q))
            terms = [[c[0]] + [g[part] for g in got] for part, c in enumerate(cut)]
        else:
            whole = [add_up(t) for t in terms]
            got = [exchange(whole, stage, q) for q in range(1, count)]
            terms = [[v] + [g[part] for g in got] for part, v in enumerate(whole)]
    kept = [add_up(t) for t in terms]
    for number in range(halvings - 1, 0, -1):
        stage = stages[number]
        got = [exchange(kept, stage, q) for q in range(1, 1 << len(stage[0][1]))]
        kept = [
            jnp.concatenate([v] + [g[part] for g in got], axis=0)
            for part, v in enumerate(kept)
        ]
    return kept, [send(v, order[0][0], order[0][1][0]) for v, order in zip(kept, orders)]


def gram_kernel(chunks, dev_ref, row_ref, keys_ref, s_hbm, *refs):
    outs, work, s_ref, sems = refs[:4], refs[4:6], refs[6], refs[7]
    tiles = s_ref.shape[1] // TILE
    spots = places(tiles)
    piece = s_ref.shape[0] // LOADS
    upper = iota((TILE, TILE), 0) <= iota((TILE, TILE), 1)
    same = iota((TILE, TILE), 0) == iota((TILE, TILE), 1)
    last = spots[1][2]
    work[1][last:, :] = jnp.zeros_like(work[1][last:, :])
    copies = []
    for q in range(LOADS):
        at = pl.ds(q * piece, piece)
        copies.append(pltpu.make_async_copy(s_hbm.at[at, :], s_ref.at[at, :], sems.at[q]))
        copies[-1].start()
    for q in range(LOADS):
        copies[q].wait()
        rows = slice(q * piece, (q + 1) * piece)
        for part in range(2):
            above, pairs, _ = spots[part]
            where = {(i, j): row for i, j, row in above}
            for band, pair_row in pairs:
                first = band * BAND * TILE
                strip = dot(s_ref[rows, first:first + BAND * TILE], s_ref[rows, first:], 0, 0)

                def tile(a, b):
                    return strip[a * TILE:(a + 1) * TILE, b * TILE:(b + 1) * TILE]

                terms = [
                    (part, where[(i, j)], tile(i - band * BAND, j - band * BAND))
                    for i in range(band * BAND, band * BAND + BAND) for j in range(i + 1, tiles)
                ]
                terms.append((part, pair_row, jnp.where(upper, tile(0, 0), tile(1, 1))))
                diagonal = jnp.sum(jnp.where(same, tile(1, 1), 0.0), axis=0, keepdims=True)
                terms.append((1, spots[1][2] + band, diagonal))
                for to, row, term in terms:
                    size = term.shape[0]
                    if q:
                        term = work[to][row:row + size, :] + term
                    work[to][row:row + size, :] = term
    base = spots[0][2]
    pivots = dev_ref.shape[0]
    sub = iota((16, s_ref.shape[1]), 0)

    for p in range(pivots):
        at = row_ref[p]
        group = pl.multiple_of((at // 16) * 16, 16)
        rows = s_ref[pl.ds(group, 16), :].astype(F32)
        wanted = jnp.where(dev_ref[p] == keys_ref[2], at - group, -1)
        row = jnp.sum(jnp.where(sub == wanted, rows, 0.0), axis=0, keepdims=True)
        for t in range(tiles):
            to = base + t * pivots + p
            work[0][to:to + 1, :] = row[:, t * TILE:(t + 1) * TILE]
    for part in range(2):
        size = work[part].shape[0] // chunks
        for q in range(chunks):
            out = outs[2 * part + q // (chunks // 2)]
            to = (q % (chunks // 2)) * size
            at = pl.multiple_of((keys_ref[part] ^ q) * size, 8)
            out[to:to + size, :] = work[part][pl.ds(at, size), :]


def local_gram(snapshots, pivot_dev, pivot_row, keys, rows, chunks):
    shapes = [jax.ShapeDtypeStruct((r // 2, TILE), F32) for r in rows for _ in range(2)]
    return pl.pallas_call(
        functools.partial(gram_kernel, chunks),
        out_shape=shapes,
        in_specs=[SMEM, SMEM, SMEM, HBM],
        out_specs=[VMEM] * 4,
        scratch_shapes=[pltpu.VMEM((r, TILE), F32) for r in rows] + [
            pltpu.VMEM(snapshots.shape, BF16),
            pltpu.SemaphoreType.DMA((LOADS,)),
        ],
        compiler_params=pltpu.CompilerParams(vmem_limit_bytes=GRANT),
        name="local_gram",
    )(in_hbm(pivot_dev), in_hbm(pivot_row), keys, in_hbm(snapshots))


def eliminate(rows, at):
    shape = rows[0].shape
    sub = iota(shape, 0)
    one = jnp.where(sub >= 0, 1.0, 0.0)

    def lane(value, j):
        return jnp.broadcast_to(value[:, j:j + 1], shape)

    def subl(value, i):
        return jnp.broadcast_to(value[i:i + 1, :], shape)

    rows = list(rows)
    count = len(rows)
    for g in range(count):
        here = rows[g]
        e = [subl(here, i) for i in range(8)]
        cols = [lane(here, at + 8 * g + j) * one for j in range(8)]
        p = [[subl(cols[j], i) if j >= i else None for j in range(8)] for i in range(8)]
        c = {h: [lane(rows[h], at + 8 * g + j) for j in range(8)] for h in range(g + 1, count)}
        scale = [None] * 8
        u = [[None] * 8 for _ in range(8)]
        for j in range(0, 8, 2):
            k = j + 1
            a, b, d = p[j][j], p[j][k], p[k][k]
            idet = 1.0 / (a * d - b * b)
            ia = 1.0 / a
            scale[j], scale[k] = ia, a * idet
            u[j][k] = b * ia
            e[k] = e[k] - u[j][k] * e[j]
            y0, y1, x0 = {}, {}, {}
            for i in range(j + 2, 8):
                y0[i] = d * p[j][i] - b * p[k][i]
                y1[i] = a * p[k][i] - b * p[j][i]
                u[j][i] = p[j][i] * ia
                u[k][i] = y1[i] * idet
                x0[i] = y0[i] * idet
            for i in range(j + 2, 8):
                for m in range(i, 8):
                    if m <= j + 3:
                        p[i][m] = p[i][m] - (y0[i] * p[j][m] + y1[i] * p[k][m]) * idet
                    else:
                        p[i][m] = p[i][m] - x0[i] * p[j][m] - u[k][i] * p[k][m]
                e[i] = e[i] - u[j][i] * e[j] - u[k][i] * e[k]
            if g + 1 < count:
                near = c[g + 1]
                z0 = (d * near[j] - b * near[k]) * idet
                z1 = (a * near[k] - b * near[j]) * idet
                rows[g + 1] = rows[g + 1] - (near[j] * ia) * e[j] - z1 * e[k]
                for m in range(j + 2, 8):
                    near[m] = near[m] - z0 * p[j][m] - z1 * p[k][m]
        if g + 2 < count:
            t = [e[i] * scale[i] for i in range(8)]
            for i in range(7, 0, -1):
                for m in range(i):
                    t[m] = t[m] - u[m][i] * t[i]
            for h in range(g + 2, count):
                rows[h] = rows[h] - add_up([c[h][j] * t[j] for j in range(8)])
        out, factor = e[0], scale[0]
        for i in range(1, 8):
            out = jnp.where(sub == i, e[i], out)
            factor = jnp.where(sub == i, scale[i], factor)
        rows[g] = out * jnp.sqrt(factor)
    return rows


def lower(value):
    return jnp.where(iota(value.shape, 1) <= iota(value.shape, 0), value, 0.0)


def product3(a, b, ca, cb):
    return dot(a[0], b[0], ca, cb) + (dot(a[0], b[1], ca, cb) + dot(a[1], b[0], ca, cb))


def twice(value):
    return tuple(jnp.concatenate([v, v], axis=0) for v in split(value))


def invert_factor(m_ref, beside=None):
    n, b = m_ref.shape[0], BLOCK
    lanes, subs = iota((b, n), 1), iota((b, n), 0)
    near, down = iota((b, TILE), 1), iota((b, TILE), 0)
    block = m_ref[:b, :TILE]
    for k in range(n // b):
        first = k * b
        tile = first // TILE * TILE
        at = first - tile
        other = b - at
        inside = (near >= at) & (near < at + b)
        eye = jnp.where(near - other == down, 1.0, 0.0)
        block = jnp.where(inside, block, eye)
        if beside is not None:
            beside(k)
        done = jnp.concatenate(
            eliminate([block[8 * g:8 * g + 8] for g in range(b // 8)], at), axis=0
        )
        inverse = split(jnp.where((near >= other) & (near - other <= down), done, 0.0))
        mine = (lanes >= first) & (lanes < first + b)
        right = m_ref[first:first + b, :]
        q = first + b
        if q < n:
            to = q // TILE * TILE
            across = product3(inverse, twice(right[:, to:to + TILE]), 1, 0)
            below = split(pltpu.roll(m_ref[q:q + b, tile:tile + TILE], b, 1))
            below = product3(below, inverse, 1, 1)
            block = m_ref[q:q + b, to:to + TILE] - product3(split(below), split(across), 1, 0)
        unit = jnp.where(lanes - first == subs, 1.0, 0.0)
        row = product3(inverse, twice(jnp.where(mine, unit, right)), 1, 0)
        m_ref[first:first + b, :] = row
        if q < n:
            high, low = split(row)
            update = dot(
                jnp.concatenate([high, high, low], axis=0),
                jnp.concatenate([high, low, high], axis=0), 0, 0)
            for r in range(q, n, b):
                m_ref[r:r + b, :] = (
                    jnp.where(mine, 0.0, m_ref[r:r + b, :]) - update[r:r + b, :]
                )


def scale_to_unit(matrix, m_ref, across_ref):
    n = matrix.shape[0]
    diagonal = jnp.where(iota((n, n), 0) == iota((n, n), 1), matrix, 0.0)
    down = lax.rsqrt(jnp.sum(diagonal, axis=1, keepdims=True))
    across = lax.rsqrt(jnp.sum(diagonal, axis=0, keepdims=True))
    m_ref[...] = matrix * down * across
    across_ref[...] = across


def solve_kernel(
    chunks, rows_total, keys_ref, start_ref, s_ref, a0_ref, a1_ref, b0_ref, b1_ref,
    modes_hbm, scores_ref, basis_ref, pa_ref, pb_ref, gh_ref, gl_ref, xh_ref, xl_ref,
    yh_ref, yl_ref, z_ref, m_ref, across_ref, factor_ref, rows_ref, high_ref, sem,
):
    packed = (pa_ref, pb_ref)
    halves = ((a0_ref, a1_ref), (b0_ref, b1_ref))
    snap, rank = start_ref.shape
    tiles = snap // TILE
    for part in range(2):
        size = packed[part].shape[0] // chunks
        for q in range(chunks):
            half = halves[part][q // (chunks // 2)]
            at = (q % (chunks // 2)) * size
            to = pl.multiple_of((keys_ref[part] ^ q) * size, 8)
            packed[part][pl.ds(to, size), :] = half[at:at + size, :]
    spots = places(tiles)

    def put(i, j, value):
        high, low = split(value)
        gh_ref[i * TILE:(i + 1) * TILE, j * TILE:(j + 1) * TILE] = high
        gl_ref[i * TILE:(i + 1) * TILE, j * TILE:(j + 1) * TILE] = low

    across, along = iota((TILE, TILE), 0), iota((TILE, TILE), 1)
    for part in range(2):
        for i, j, row in spots[part][0]:
            value = packed[part][row:row + TILE, :]
            put(i, j, value)
            put(j, i, jnp.transpose(value))
        for band, row in spots[part][1]:
            value = packed[part][row:row + TILE, :]
            turned = jnp.transpose(value)
            end = spots[1][2] + band
            diagonal = jnp.where(across == along, pb_ref[end:end + 1, :], turned)
            i = band * BAND
            put(i, i, jnp.where(across <= along, value, turned))
            put(i + 1, i + 1, jnp.where(across > along, value, diagonal))
    strips = rank // BLOCK
    step = snap // strips

    def product(at, xh, xl):
        gh = gh_ref[at, :]
        return dot(gh, xh, 1, 0) + (dot(gh, xl, 1, 0) + dot(gl_ref[at, :], xh, 1, 0))

    yh_ref[...], yl_ref[...] = split(start_ref[...])
    for r in range(strips):
        at = pl.ds(r * step, step)
        z_ref[at, :] = product(at, yh_ref[...], yl_ref[...])
    square = 0.0
    for r in range(strips):
        at = pl.ds(r * step, step)
        yh, yl = split(z_ref[at, :])
        yh_ref[at, :], yl_ref[at, :] = yh, yl
        square = square + dot(yh, yh, 0, 0)
    scale_to_unit(square, m_ref, across_ref)

    def iteration(number, carry):
        def beside(k):
            at = pl.ds(k * step, step)
            z_ref[at, :] = product(at, yh_ref[...], yl_ref[...])

        invert_factor(m_ref, beside)
        factor_ref[...] = (lower(m_ref[...]) * across_ref[...]).astype(BF16)

        @pl.when(number == ITERS - 1)
        def _():
            factor = factor_ref[...]
            iterate = dot(yh_ref[...], factor, 1, 1) + dot(yl_ref[...], factor, 1, 1)
            xh_ref[...], xl_ref[...] = split(iterate)

        factor = factor_ref[...]
        square = 0.0
        for r in range(strips):
            at = pl.ds(r * step, step)
            zh, zl = split(z_ref[at, :])
            yh, yl = split(dot(zh, factor, 1, 1) + dot(zl, factor, 1, 1))
            yh_ref[at, :], yl_ref[at, :] = yh, yl
            square = square + dot(yh, yh, 0, 0)
        scale_to_unit(square, m_ref, across_ref)
        return carry

    lax.fori_loop(0, ITERS, iteration, 0)
    yh, yl = yh_ref[...], yl_ref[...]
    xh, xl = xh_ref[...], xl_ref[...]
    small = dot(xh, yh, 0, 0) + (dot(xh, yl, 0, 0) + dot(xl, yh, 0, 0))
    scale_to_unit((small + jnp.transpose(small)) * (0.5 / rows_total), m_ref, across_ref)
    invert_factor(m_ref)
    fh, fl = split(lower(m_ref[...]) * across_ref[...])
    coef = (dot(xh, fh, 1, 1) + (dot(xh, fl, 1, 1) + dot(xl, fh, 1, 1))).astype(BF16)
    chunk = 512
    spans = [pl.ds(r * chunk, chunk) for r in range(s_ref.shape[0] // chunk)]
    for at in spans:
        basis = dot(s_ref[at, :], coef, 1, 0)
        rows_ref[at, :] = basis
        high_ref[at, :] = basis.astype(BF16)
    base = spots[0][2]
    pivots = basis_ref.shape[0]
    picked = jnp.concatenate(
        [pa_ref[base + t * pivots:base + (t + 1) * pivots, :] for t in range(tiles)], axis=1
    )
    panel = dot(picked.astype(BF16), coef, 1, 0)
    gram = dot(panel, panel, 1, 1, HIGHEST)
    same = iota((pivots, pivots), 0) == iota((pivots, pivots), 1)
    diagonal = jnp.where(same, gram, 0.0)
    down = lax.rsqrt(jnp.sum(diagonal, axis=1, keepdims=True))
    across = lax.rsqrt(jnp.sum(diagonal, axis=0, keepdims=True))
    wide = jnp.concatenate(
        [gram * down * across, jnp.where(same, 1.0, 0.0)]
        + [jnp.zeros((pivots, TILE - 2 * pivots), F32)], axis=1
    )
    done = eliminate([wide[8 * g:8 * g + 8] for g in range(pivots // 8)], 0)
    factor = lower(jnp.concatenate(done, axis=0)[:, pivots:2 * pivots]) * across
    turned = dot(factor, panel, 1, 0, HIGHEST)
    basis_ref[...] = turned
    th, tl = split(turned)
    thrice_h = jnp.concatenate([th, th, th], axis=0)
    thrice_l = jnp.concatenate([tl, tl, tl], axis=0)
    stacked = jnp.concatenate([th, tl, th], axis=0)
    from_low = iota((chunk, 3 * pivots), 1) >= 2 * pivots
    ones = jnp.ones((8, rank), BF16)
    store = pltpu.make_async_copy(high_ref, modes_hbm, sem)
    store.start()

    def project(r, carry):
        at = pl.ds(pl.multiple_of(r * chunk, chunk), chunk)
        basis, high = rows_ref[at, :], high_ref[at, :]
        coeffs = dot(high, thrice_h, 1, 1) + dot(high, thrice_l, 1, 1)
        ch, cl = split(coeffs)
        left = basis - dot(jnp.where(from_low, cl, ch), stacked, 1, 0)
        qh, ql = split(left * left)
        total = (dot(ones, qh, 1, 1) + dot(ones, ql, 1, 1)) * (1.0 / rank)
        scores_ref[:, at] = total[0:1, :]
        return carry

    lax.fori_loop(0, len(spans), project, 0, unroll=2)
    store.wait()


def solve(snapshots, start, keys, pieces, pivots, rows, chunks, rows_total):
    snap, rank = start.shape
    here = snapshots.shape[0]
    return pl.pallas_call(
        functools.partial(solve_kernel, chunks, rows_total),
        out_shape=[
            jax.ShapeDtypeStruct((here, rank), BF16),
            jax.ShapeDtypeStruct((1, here), F32),
            jax.ShapeDtypeStruct((pivots, rank), F32),
        ],
        in_specs=[SMEM] + [VMEM] * 6,
        out_specs=[HBM, VMEM, VMEM],
        scratch_shapes=[pltpu.VMEM((r, TILE), F32) for r in rows] + [
            pltpu.VMEM((snap, snap), BF16),
            pltpu.VMEM((snap, snap), BF16),
            pltpu.VMEM((snap, rank), BF16),
            pltpu.VMEM((snap, rank), BF16),
            pltpu.VMEM((snap, rank), BF16),
            pltpu.VMEM((snap, rank), BF16),
            pltpu.VMEM((snap, rank), F32),
            pltpu.VMEM((rank, rank), F32),
            pltpu.VMEM((1, rank), F32),
            pltpu.VMEM((rank, rank), BF16),
            pltpu.VMEM((here, rank), F32),
            pltpu.VMEM((here, rank), BF16),
            pltpu.SemaphoreType.DMA,
        ],
        compiler_params=pltpu.CompilerParams(vmem_limit_bytes=GRANT),
        name="solve",
    )(keys, start, snapshots, *pieces)


def local(mesh_shape, snapshots, start, pivot_dev, pivot_row):
    here, snap = snapshots.shape
    pivots = pivot_dev.shape[0]
    rows = part_rows(snap // TILE, pivots)
    orders, halvings = exchange_plan(mesh_shape, rows)
    chunks = chunks_of(orders[0], halvings)
    myself = lax.axis_index(("grp", "blk"))
    keys = jnp.stack([key_of(orders[0], halvings), key_of(orders[1], halvings), myself])
    a0, a1, b0, b1 = local_gram(snapshots, pivot_dev, pivot_row, keys, rows, chunks)
    own, other = reduce_parts([a0, b0], [a1, b1], orders, halvings)
    pieces = (own[0], other[0], own[1], other[1])
    rows_total = here * mesh_shape["grp"] * mesh_shape["blk"]
    modes, scores, basis = solve(
        snapshots, start, keys, pieces, pivots, rows, chunks, rows_total
    )
    return modes, scores.reshape(here), basis.T


def solution(mesh):
    placed = (P(("grp", "blk"), None), P(), P(), P())

    def body(*args):
        return local(dict(mesh.shape), *args)

    return jax.shard_map(
        body,
        mesh=mesh,
        in_specs=placed,
        out_specs=(P(("grp", "blk"), None), P(("grp", "blk")), P()),
        check_vma=False,
    )
```
